32 devices in a mesh: dec: 8 (over z, x), ra: 4 (over y, core).
Axes of the slice: x: 2, y: 2, z: 4, core: 2. Of those that a mesh axis runs over, the one named last changes fastest.
Arguments:
- split_maps: bfloat16 [6, 2048, 1024], P(None, 'dec', 'ra'), may hold values from -40 to 40
- white_noise: bfloat16 [4096, 2048], P('dec', 'ra'), may hold values from -6 to 6
Outputs:
- noise_realization: float32 [2048, 1024], P('dec', 'ra')
The draws below stay inside these ranges and needn't reach their ends.
All inputs are finite; a program needn't handle non-finite values.
Results may differ from the reference program's by a relative error of at most 0.0035.
The reference program's roundings to bfloat16 on the way (of `differ`) count: a program that leaves them out, or rounds other values in their place, can miss the bound.
Values may be sent and summed in bfloat16 or wider, within the bound.
A program may use at most 64 MiB of HBM per device.

```python
import jax
import jax.numpy as jnp
from jax import lax

CORE = 256
SPLITS = 6
SMOOTH = 4
EXT = 512
NDEC = 2048
NRA = 1024
N_DEC = 8
N_RA = 4


def split_waves(key, count):
    subkeys = jax.random.split(key, 3)
    periods = CORE * jnp.exp(jax.random.uniform(subkeys[0], (SPLITS, 2), jnp.float32, jnp.log(2.0), jnp.log(6.0)))
    offsets = jax.random.uniform(subkeys[1], (SPLITS, 2), jnp.float32, 0.0, 2.0 * jnp.pi)
    heights = jax.random.uniform(subkeys[2], (SPLITS, 2), jnp.float32, 2.5, 5.0)
    places = jnp.arange(count, dtype=jnp.float32)
    phases = 2.0 * jnp.pi * places[None, None, :] / periods[:, :, None] + offsets[:, :, None]
    return jnp.sum(heights[:, :, None] * jnp.sin(phases), axis=1)


def draw_split_maps(key, part):
    subkeys = jax.random.split(key, 6)
    block_side = CORE // 4
    low_level, high_level = (0.4, 2.5)
    levels = jnp.exp(jax.random.uniform(subkeys[0], (NDEC // block_side, NRA // block_side), jnp.float32, jnp.log(low_level), jnp.log(high_level)))
    levels = jnp.repeat(jnp.repeat(levels, block_side, axis=0), block_side, axis=1)
    pixel_scale = jnp.exp(jax.random.uniform(subkeys[1], (NDEC, NRA), jnp.float32, jnp.log(0.7), jnp.log(1.4)))
    white_part = jax.random.normal(subkeys[2], (SPLITS, NDEC, NRA), jnp.float32)
    signal = 2.0 * jax.random.normal(subkeys[3], (NDEC, NRA), jnp.float32)
    banded = white_part + 0.8 * jnp.roll(white_part, 1, axis=2)
    along_rows = split_waves(subkeys[4], NDEC)
    along_cols = split_waves(subkeys[5], NRA)
    drifts = along_rows[:, :, None] + along_cols[:, None, :]
    values = signal[None] + drifts + (levels * pixel_scale)[None] * banded
    return jnp.clip(values, -40.0, 40.0).astype(jnp.bfloat16)


def shard_levels(rng, shape, cuts, least, high):
    loudness, own = 1.0, jax.random.fold_in(rng, 6)
    for dim, shards_of in cuts:
        steps = jnp.exp(jax.random.uniform(jax.random.fold_in(own, dim), (shards_of,), jnp.float32, least / len(cuts), high / len(cuts)))
        loudness = loudness * jnp.repeat(steps, shape[dim] // shards_of).reshape([-1 if axis == dim else 1 for axis in range(len(shape))])
    return loudness


def bell_draw(own_key, dims, width, limit, cuts=(), kind=jnp.bfloat16):
    values = jax.random.normal(own_key, dims, jnp.float32) * width
    if len(cuts) > 0:
        values = shard_levels(own_key, dims, cuts, -0.22, 0.18) * values
    return jnp.clip(values, min=-limit, max=limit).astype(kind)


def setup_inputs(seed: int = 0) -> dict:
    streams_of = jax.random.split(jax.random.key(seed), 3)
    return {
        "split_maps": draw_split_maps(jax.random.fold_in(streams_of[2], 71), 0),
        "white_noise": bell_draw(streams_of[1], (EXT * N_DEC, EXT * N_RA), 1.0, 6.0, ((0, 8), (1, 4))),
    }


def make_tables(length):
    indices = jnp.arange(length, dtype=jnp.int32)
    phases = indices[:, None] * indices[None, :] % length
    angles = phases.astype(jnp.float32) * (2.0 * jnp.pi / length)
    cos_table = jnp.cos(angles).astype(jnp.bfloat16)
    sin_table = jnp.sin(angles).astype(jnp.bfloat16)
    forward_left = jnp.concatenate([cos_table, sin_table], axis=0)
    forward_right = jnp.concatenate([jnp.concatenate([cos_table, -sin_table], axis=1), jnp.concatenate([-sin_table, -cos_table], axis=1)], axis=0)
    inverse_left = jnp.concatenate([jnp.concatenate([cos_table, -sin_table], axis=1), jnp.concatenate([sin_table, cos_table], axis=1)], axis=0)
    inverse_right = jnp.concatenate([cos_table, -sin_table], axis=0)
    profile = jnp.sin(jnp.pi * (indices.astype(jnp.float32) + 0.5) / length) ** 2
    window = profile[:, None] * profile[None, :]
    distance = jnp.abs(indices[:, None] - indices[None, :])
    distance = jnp.minimum(distance, length - distance)
    smoother = jnp.where(distance <= SMOOTH, 1.0 / (2 * SMOOTH + 1), 0.0).astype(jnp.float32)
    return (forward_left, forward_right, inverse_left, inverse_right, window, smoother)

def forward(tile, forward_left, forward_right):
    length = tile.shape[0]
    halves = jnp.dot(forward_left, tile, preferred_element_type=jnp.float32).astype(jnp.bfloat16)
    joined = jnp.concatenate([halves[:length], halves[length:]], axis=1)
    return jnp.dot(joined, forward_right, preferred_element_type=jnp.float32)

def tile_model(extended, noise_tile, tables):
    forward_left, forward_right, inverse_left, inverse_right, window, smoother = tables
    length = noise_tile.shape[0]
    splits = extended.shape[0]
    coadded = lax.optimization_barrier(jnp.mean(extended.astype(jnp.float32), axis=0))

    def accumulate(number, summed):
        member = lax.dynamic_index_in_dim(extended, number, 0, keepdims=False)
        differ = (window * (member.astype(jnp.float32) - coadded)).astype(jnp.bfloat16)
        spectra = forward(differ, forward_left, forward_right)
        return summed + spectra[:, :length] ** 2 + spectra[:, length:] ** 2
    spectrum_power = lax.fori_loop(0, splits, accumulate, jnp.zeros((length, length), jnp.float32))
    spectrum_power = spectrum_power / ((splits - 1) * jnp.sum(window * window))
    smooth = jnp.dot(jnp.dot(smoother, spectrum_power, precision=lax.Precision.HIGHEST), smoother, precision=lax.Precision.HIGHEST)
    filter_gain = jnp.sqrt(smooth)
    spectra = forward(noise_tile, forward_left, forward_right)
    shaped = jnp.concatenate([filter_gain * spectra[:, :length], filter_gain * spectra[:, length:]], axis=0).astype(jnp.bfloat16)
    mixture = jnp.dot(inverse_left, shaped, preferred_element_type=jnp.float32).astype(jnp.bfloat16)
    joined = jnp.concatenate([mixture[:length], mixture[length:]], axis=1)
    real_part = jnp.dot(joined, inverse_right, preferred_element_type=jnp.float32)
    return window * real_part / (length * length)

def reference(split_maps, white_noise):
    splits = split_maps.shape[0]
    margin = CORE // 2
    length = 2 * CORE
    tables = make_tables(length)
    padded = jnp.pad(split_maps, ((0, 0), (margin, margin), (margin, margin)))
    tile_rows = split_maps.shape[1] // CORE
    tile_cols = split_maps.shape[2] // CORE
    anchor = jnp.zeros((), jnp.int32)

    def one_tile(position):
        tile_row = (position // tile_cols).astype(jnp.int32)
        tile_col = (position % tile_cols).astype(jnp.int32)
        extended = lax.dynamic_slice(padded, (anchor, tile_row * CORE, tile_col * CORE), (splits, length, length))
        noise_tile = lax.dynamic_slice(white_noise, (tile_row * length, tile_col * length), (length, length))
        return tile_model(extended, noise_tile, tables)
    results = lax.map(one_tile, jnp.arange(tile_rows * tile_cols, dtype=jnp.int32))
    results = results.reshape(tile_rows, tile_cols, 2, CORE, 2, CORE)
    summed = jnp.zeros((tile_rows + 1, CORE, tile_cols + 1, CORE), jnp.float32)
    for row_half in range(2):
        for col_half in range(2):
            quarter = results[:, :, row_half, :, col_half, :].transpose(0, 2, 1, 3)
            summed = summed + jnp.pad(quarter, ((row_half, 1 - row_half), (0, 0), (col_half, 1 - col_half), (0, 0)))
    summed = summed.reshape((tile_rows + 1) * CORE, (tile_cols + 1) * CORE)
    return summed[margin:margin + tile_rows * CORE, margin:margin + tile_cols * CORE]
```

```python
import functools

import jax
import jax.numpy as jnp
import numpy as np
from jax import lax
from jax.experimental import pallas as pl
from jax.experimental.pallas import tpu as pltpu
from jax.sharding import PartitionSpec as P

SMOOTH = 4
MESH = pl.DeviceIdType.MESH
F32 = jnp.float32
BF16 = jnp.bfloat16
PAD = 16


def make_constants(length):
    half = length // 2
    indices = np.arange(length)
    angles = (indices[:, None] * indices[None, :] % length) * (2.0 * np.pi / length)
    cos_table, sin_table = np.cos(angles), np.sin(angles)
    packed = np.concatenate([cos_table[: half + 1], sin_table[1:half]], axis=0)
    profile = np.sin(np.pi * (indices + 0.5) / length) ** 2
    distance = np.abs(indices[:, None] - indices[None, :])
    near = (np.minimum(distance, length - distance) <= SMOOTH).astype(np.float64)
    mirrored = near[:, (-indices) % length]
    even = (near + mirrored)[: half + 1, :half]
    even[:, 0] = near[: half + 1, 0]
    odd = (near - mirrored)[:half, :half]
    odd[0, :] = 0.0
    odd[:, 0] = 0.0
    even_rows = np.zeros((half + PAD, half))
    even_rows[: half + 1] = even
    even_cols = np.zeros((half, half + 128))
    even_cols[:, : half + 1] = even.T
    edge = np.zeros((half + 128,))
    edge[: half + 1] = near[: half + 1, half]
    return dict(
        packed=packed, profile=profile, even_rows=even_rows, even_cols=even_cols, odd=odd,
        edge=edge, total=float(np.sum(profile**2) ** 2),
    )


def dot(left, right):
    return jnp.dot(left, right, preferred_element_type=F32)


def parts_of(values):
    high = values.astype(BF16)
    return high, (values - high.astype(F32)).astype(BF16)


def fine_left(matrix, values):
    high, low = parts_of(values)
    return dot(matrix, high) + dot(matrix, low)


def fine_right(values, matrix):
    high, low = parts_of(values)
    return dot(high, matrix) + dot(low, matrix)


def contrast(number, planes):
    if number < 3:
        return planes[2 * number] - planes[2 * number + 1]
    pair = [planes[2 * i] + planes[2 * i + 1] for i in range(3)]
    return pair[0] - pair[1] if number == 3 else pair[0] + pair[1] - 2.0 * pair[2]


WEIGHTS = (0.5, 0.5, 0.5, 0.25, 1.0 / 12.0)
PLANES = 5


def gains(squares, cross, even_rows, even_cols, odd, edge_rows, edge_cols, scale):
    half = cross.shape[0]
    rows = lax.broadcasted_iota(jnp.int32, (half, half), 0)
    cols = lax.broadcasted_iota(jnp.int32, (half, half), 1)
    a, b = squares[:half, :half], squares[:half, half:]
    d, e = squares[half:, :half], squares[half:, half:]
    inner_row, inner_col = rows > 0, cols > 0
    zero = jnp.zeros_like(a)
    e_col = jnp.where(inner_col, e, zero)
    top = a + jnp.where(inner_col, b, zero) + jnp.where(inner_row, d + e_col, zero)
    last_col = b + jnp.where(inner_row, e, zero)
    last_row = jnp.concatenate([(d + e_col)[:1], e[:1, :128]], axis=1)
    wide = jnp.concatenate([top, last_col[:, :128]], axis=1)
    once = fine_left(even_rows, wide) + edge_rows * last_row
    smooth = fine_right(once[:, :half], even_cols) + once[:, half : half + 1] * edge_cols
    twist = jnp.where(inner_row & inner_col, cross, zero)
    turned = fine_right(fine_left(odd, twist), odd)
    root = lambda values: jnp.sqrt(jnp.maximum(values * scale, 0.0))
    even = smooth[:half, :half]
    return (
        root(even + turned), root(even - turned),
        root(smooth[half : half + 1, :half]), root(smooth[:half, half : half + 1]),
        root(smooth[half : half + 1, half : half + 1]),
    )


def shaped(noise, plus, minus, last_row, last_col, corner):
    half = plus.shape[0]
    rows = lax.broadcasted_iota(jnp.int32, (half, half), 0)
    cols = lax.broadcasted_iota(jnp.int32, (half, half), 1)
    first_row, first_col = rows == 0, cols == 0
    either, both = first_row | first_col, first_row & first_col
    rounded = lambda values: values.astype(BF16).astype(F32)
    a, b = noise[:half, :half], noise[:half, half:]
    d, e = noise[half:, :half], noise[half:, half:]
    re_plus, re_minus = rounded(plus * (a - e)), rounded(minus * (a + e))
    im_plus, im_minus = rounded(plus * (b + d)), rounded(minus * (b - d))
    times = jnp.where(both, 1.0, 2.0)
    row_gain = jnp.where(first_row, last_row, plus)
    col_gain = jnp.where(first_col, last_col, plus)
    end_gain = jnp.where(both, corner, jnp.where(first_row, last_row, last_col))
    pick = lambda gain, block, inner: jnp.where(either, times * rounded(gain * block), 2.0 * inner)
    rest = lambda inner: jnp.where(either, 0.0, 2.0 * inner)
    joined = lambda z00, z01, z10, z11: jnp.concatenate(
        [jnp.concatenate([z00, z01], axis=1), jnp.concatenate([z10, z11], axis=1)], axis=0
    ).astype(BF16)
    first = joined(
        pick(plus, a, re_plus), pick(col_gain, b, im_plus),
        pick(row_gain, d, im_plus), pick(end_gain, e, -re_plus),
    )
    return first, joined(rest(re_minus), rest(im_minus), rest(-im_minus), rest(re_minus))


def kernel(
    n_dec, n_ra, scale,
    maps_hbm, noise_hbm, table_hbm, turned_hbm, rows_hbm, cols_hbm, odd_hbm,
    tall_hbm, wide_hbm, edge_rows_hbm, edge_cols_hbm,
    out_ref,
    maps, noise, table, turned, even_rows, even_cols, odd,
    tall_ref, wide_ref, edge_rows_ref, edge_cols_ref,
    ext, window, squares, cross, spectrum, real, strip_out, strip_in, row_out, row_in,
    local_sem, send_sem, recv_sem, fold_send, fold_recv,
):
    dec, ra = lax.axis_index("dec"), lax.axis_index("ra")
    length = noise.shape[0]
    core = length // 2
    margin = core // 2
    half = core
    low, mid, high = pl.ds(0, margin), pl.ds(margin, core), pl.ds(margin + core, margin)
    head, tail = pl.ds(margin, margin), pl.ds(core, margin)
    exists = {"up": dec > 0, "down": dec < n_dec - 1, "left": ra > 0, "right": ra < n_ra - 1}
    target = {
        "up": {"dec": dec - 1}, "down": {"dec": dec + 1},
        "left": {"ra": ra - 1}, "right": {"ra": ra + 1},
    }
    opposite = {"up": "down", "down": "up", "left": "right", "right": "left"}

    pairs = [
        pltpu.make_async_copy(maps_hbm.at[pl.ds(2 * i, 2)], maps.at[pl.ds(2 * i, 2)], local_sem.at[i])
        for i in range(3)
    ]
    loads = [
        pltpu.make_async_copy(source, place, local_sem.at[3 + number])
        for number, (source, place) in enumerate(
            [(tall_hbm, tall_ref), (wide_hbm, wide_ref), (noise_hbm, noise), (table_hbm, table),
             (turned_hbm, turned), (rows_hbm, even_rows), (cols_hbm, even_cols), (odd_hbm, odd),
             (edge_rows_hbm, edge_rows_ref), (edge_cols_hbm, edge_cols_ref)]
        )
    ]
    for load in pairs:
        load.start()

    barrier = pltpu.get_barrier_semaphore()
    for way in exists:
        @pl.when(exists[way])
        def _(way=way):
            pl.semaphore_signal(barrier, inc=1, device_id=target[way], device_id_type=MESH)
    inner = pl.ds(1, 2)
    moves = [
        ("up", head, 1, high, 1), ("down", tail, 1, low, 1),
        ("up", head, 2, high, 2), ("down", tail, 2, low, 2),
        ("left", mid, 1, mid, 3), ("right", mid, 2, mid, 0),
        ("left", high, 1, high, 3), ("left", low, 1, low, 3),
        ("right", high, 2, high, 0), ("right", low, 2, low, 0),
    ]

    def move(plane, number):
        way, rows, blocks, to_rows, to_blocks = moves[number]
        return pltpu.make_async_remote_copy(
            src_ref=ext.at[plane, blocks, rows, :],
            dst_ref=ext.at[plane, to_blocks, to_rows, :],
            send_sem=send_sem.at[plane, number],
            recv_sem=recv_sem.at[plane, number],
            device_id=target[way],
            device_id_type=MESH,
        )

    def start(plane, numbers):
        for number in numbers:
            @pl.when(exists[moves[number][0]])
            def _(number=number):
                move(plane, number).start()

    def wait_recv(plane, numbers):
        for number in numbers:
            @pl.when(exists[opposite[moves[number][0]]])
            def _(number=number):
                move(plane, number).wait_recv()

    def wait_send(plane, numbers):
        for number in numbers:
            @pl.when(exists[moves[number][0]])
            def _(number=number):
                move(plane, number).wait_send()

    for plane in range(PLANES):
        if plane < 3:
            pairs[plane].wait()
        used = range(6) if plane >= 3 else range(2 * plane, 2 * plane + 2)
        values = contrast(plane, {s: maps[s].astype(F32) for s in used}).astype(BF16)
        ext[plane, 1, mid, :] = values[:, :margin]
        ext[plane, 2, mid, :] = values[:, margin:]
        if plane == 0:
            pl.semaphore_wait(barrier, sum(here.astype(jnp.int32) for here in exists.values()))
        start(plane, (0, 1, 2, 3, 4, 5))

    for load in loads:
        load.start()
    whole = pl.ds(0, length)
    for way, rows, blocks in (
        ("up", low, inner), ("down", high, inner), ("left", whole, pl.ds(0, 1)), ("right", whole, pl.ds(3, 1)),
    ):
        @pl.when(jnp.logical_not(exists[way]))
        def _(rows=rows, blocks=blocks):
            ext[:, blocks, rows, :] = jnp.zeros((PLANES, blocks.size, rows.size, margin), BF16)

    for load in loads:
        load.wait()
    window[...] = tall_ref[...] * wide_ref[...]
    squares[...] = jnp.zeros_like(squares)
    cross[...] = jnp.zeros_like(cross)

    def transform(tile):
        return dot(dot(table[...], tile).astype(BF16), turned[...])

    spectrum[...] = transform(noise[...])

    def forward_corners(plane):
        for number in range(4):
            wait_recv(plane, (number,))
            start(plane, (6 + number,))

    def windowed(plane, rows, blocks):
        tile = jnp.concatenate([ext[plane, block, rows, :] for block in blocks], axis=1)
        shape = jnp.concatenate(
            [window[rows, block * margin : (block + 1) * margin] for block in blocks], axis=1
        )
        return (shape * tile.astype(F32)).astype(BF16)

    def gather_power(plane):
        wait_recv(plane, range(4, 10))
        add_power(plane, transform(windowed(plane, whole, range(4))))

    def gather_last(plane):
        halves = dot(table[...], windowed(plane, whole, (1, 2))).astype(BF16)
        spectrum_mid = dot(halves, turned[mid, :])
        wait_recv(plane, (4, 5))
        sides = dot(table[:, mid], windowed(plane, mid, (0, 3)))
        wait_recv(plane, range(6, 10))
        sides = sides + dot(table[:, low], windowed(plane, low, (0, 3)))
        sides = (sides + dot(table[:, high], windowed(plane, high, (0, 3)))).astype(BF16)
        add_power(
            plane,
            spectrum_mid + dot(sides[:, :margin], turned[low, :]) + dot(sides[:, margin:], turned[high, :]),
        )

    def add_power(plane, values):
        weight = jnp.where(
            plane < 3, WEIGHTS[0], jnp.where(plane == 3, WEIGHTS[3], WEIGHTS[4])
        ).astype(F32)
        squares[...] += values * values * weight
        a, b = values[:half, :half], values[:half, half:]
        d, e = values[half:, :half], values[half:, half:]
        cross[...] += (b * d - a * e) * (2.0 * weight)

    forward_corners(0)

    def step(plane, carry):
        forward_corners(plane)
        gather_power(plane - 1)
        return carry

    lax.fori_loop(1, PLANES, step, 0)
    gather_last(PLANES - 1)

    filters = gains(
        squares[...], cross[...], even_rows[...], even_cols[...], odd[...],
        edge_rows_ref[...], edge_cols_ref[...], scale,
    )
    mixed, mirrored = shaped(spectrum[...], *filters)

    def inverse(rows):
        return (dot(turned[rows, :], mixed) + dot(turned[rows, :], mirrored)).astype(BF16)

    def synthesize(part, rows, cols):
        real[rows, cols] = window[rows, cols] * dot(part, table[:, cols])

    def strip(side, rows, number):
        return pltpu.make_async_remote_copy(
            src_ref=strip_out.at[side, rows, :],
            dst_ref=strip_in.at[side, rows, :],
            send_sem=fold_send.at[side, number],
            recv_sem=fold_recv.at[side, number],
            device_id=target[("left", "right")[side]],
            device_id_type=MESH,
        )

    def band(side):
        return pltpu.make_async_remote_copy(
            src_ref=row_out.at[side],
            dst_ref=row_in.at[side],
            send_sem=fold_send.at[side, 3],
            recv_sem=fold_recv.at[side, 3],
            device_id=target[("up", "down")[side]],
            device_id_type=MESH,
        )

    pieces = ((low, 0), (high, 1), (mid, 2))
    ways = ("left", "right")
    def send_strips(part, rows, number):
        for side, cols in enumerate((low, high)):
            values = window[rows, cols] * dot(part, table[:, cols])
            strip_out[side, rows, :] = values.astype(BF16)
            @pl.when(exists[ways[side]])
            def _(side=side, rows=rows, number=number):
                strip(side, rows, number).start()

    outer = [inverse(rows) for rows, number in pieces[:2]]
    for part, (rows, number) in zip(outer, pieces):
        send_strips(part, rows, number)
    middle = inverse(mid)
    send_strips(middle, *pieces[2])
    for part, (rows, number) in zip(outer + [middle], pieces):
        synthesize(part, rows, mid)

    def fold_columns(rows, number):
        for side, cols in ((1, head), (0, tail)):
            @pl.when(exists[opposite[ways[side]]])
            def _(side=side, cols=cols):
                strip(side, rows, number).wait_recv()
                real[rows, cols] += strip_in[side, rows, :].astype(F32)

    for side, (rows, number) in enumerate(pieces[:2]):
        fold_columns(rows, number)
        row_out[side] = real[rows, mid].astype(BF16)
        @pl.when(exists[("up", "down")[side]])
        def _(side=side):
            band(side).start()
    fold_columns(*pieces[2])
    for side, rows in ((1, head), (0, tail)):
        @pl.when(exists[("down", "up")[side]])
        def _(side=side, rows=rows):
            band(side).wait_recv()
            real[rows, mid] += row_in[side].astype(F32)
    out_ref[...] = real[mid, mid]

    def drain(plane, carry):
        wait_send(plane, range(10))
        return carry

    lax.fori_loop(0, PLANES, drain, 0)
    for side in range(2):
        @pl.when(exists[ways[side]])
        def _(side=side):
            for rows, number in pieces:
                strip(side, rows, number).wait_send()

        @pl.when(exists[("up", "down")[side]])
        def _(side=side):
            band(side).wait_send()


def shards(n_dec, n_ra, constants, split_maps, white_noise):
    splits, core = split_maps.shape[0], split_maps.shape[1]
    length, half, margin = 2 * core, core, core // 2
    as_bf16 = lambda values: jnp.asarray(np.asarray(values, np.float32).astype(jnp.bfloat16))
    as_f32 = lambda values: jnp.asarray(np.asarray(values, np.float32))
    packed = as_bf16(constants["packed"])
    turned = as_bf16(constants["packed"].T)
    edge = constants["edge"]
    scale = 1.0 / ((splits - 1) * constants["total"] * (2 * SMOOTH + 1) ** 2)
    in_vmem = pl.BlockSpec(memory_space=pltpu.VMEM)
    in_hbm = pl.BlockSpec(memory_space=pl.ANY)
    result = pl.pallas_call(
        functools.partial(kernel, n_dec, n_ra, scale),
        out_shape=pltpu.VMEM((core, core), F32),
        in_specs=[in_hbm] * 11,
        out_specs=in_vmem,
        scratch_shapes=[
            pltpu.VMEM((splits, core, core), BF16),
            pltpu.VMEM((length, length), BF16),
            pltpu.VMEM((length, length), BF16),
            pltpu.VMEM((length, length), BF16),
            pltpu.VMEM((half + PAD, half), BF16),
            pltpu.VMEM((half, half + 128), BF16),
            pltpu.VMEM((half, half), BF16),
            pltpu.VMEM((length, 1), F32),
            pltpu.VMEM((1, length), F32),
            pltpu.VMEM((half + PAD, 1), F32),
            pltpu.VMEM((1, half + 128), F32),
            pltpu.VMEM((PLANES, 4, length, margin), BF16),
            pltpu.VMEM((length, length), F32),
            pltpu.VMEM((length, length), F32),
            pltpu.VMEM((half, half), F32),
            pltpu.VMEM((length, length), F32),
            pltpu.VMEM((length, length), F32),
            pltpu.VMEM((2, length, margin), BF16),
            pltpu.VMEM((2, length, margin), BF16),
            pltpu.VMEM((2, margin, core), BF16),
            pltpu.VMEM((2, margin, core), BF16),
            pltpu.SemaphoreType.DMA((13,)),
            pltpu.SemaphoreType.DMA((PLANES, 10)),
            pltpu.SemaphoreType.DMA((PLANES, 10)),
            pltpu.SemaphoreType.DMA((2, 4)),
            pltpu.SemaphoreType.DMA((2, 4)),
        ],
        compiler_params=pltpu.CompilerParams(
            collective_id=0, has_side_effects=True, vmem_limit_bytes=56 << 20
        ),
    )(
        split_maps, white_noise, packed, turned,
        as_bf16(constants["even_rows"]), as_bf16(constants["even_cols"]), as_bf16(constants["odd"]),
        as_f32(constants["profile"][:, None]), as_f32(constants["profile"][None, :]),
        as_f32(edge[: half + PAD, None]), as_f32(edge[None, :]),
    )
    return result * (1.0 / (length * length))


def solution(mesh):
    n_dec, n_ra = mesh.shape["dec"], mesh.shape["ra"]

    def body(split_maps, white_noise):
        constants = make_constants(2 * split_maps.shape[1])
        return shards(n_dec, n_ra, constants, split_maps, white_noise)

    placed = (P(None, "dec", "ra"), P("dec", "ra"))
    return jax.shard_map(
        body, mesh=mesh, in_specs=placed, out_specs=P("dec", "ra"), check_vma=False
    )
```

```python
import functools

import jax
import jax.numpy as jnp
import numpy as np
from jax import lax
from jax.experimental import pallas as pl
from jax.experimental.pallas import tpu as pltpu
from jax.sharding import PartitionSpec as P

SMOOTH = 4
MESH = pl.DeviceIdType.MESH
F32 = jnp.float32
BF16 = jnp.bfloat16
PAD = 16


def make_constants(length):
    half = length // 2
    indices = np.arange(length)
    angles = (indices[:, None] * indices[None, :] % length) * (2.0 * np.pi / length)
    cos_table, sin_table = np.cos(angles), np.sin(angles)
    packed = np.concatenate([cos_table[: half + 1], sin_table[1:half]], axis=0)
    profile = np.sin(np.pi * (indices + 0.5) / length) ** 2

    def near(left, right):
        distance = np.abs(left[:, None] - right[None, :]) % length
        return (np.minimum(distance, length - distance) <= SMOOTH).astype(np.float64)

    signed = np.concatenate([np.arange(half + 1), -np.arange(1, half)])
    kept = np.arange(half + PAD)
    smooth_rows = near(kept, np.arange(half)) * (kept <= half)[:, None]
    first = np.arange(PAD)
    fold_first = near(first, -first) * (first > 0)[None, :]
    last = half - PAD + np.arange(2 * PAD)
    fold_last = np.zeros((2 * PAD, 2 * PAD))
    fold_last[:, :PAD] = near(last, -last[:PAD])
    fold_last[:, PAD] = near(last, np.array([half]))[:, 0]
    fold_last[last > half] = 0.0
    return dict(
        packed=packed, profile=profile, smooth_cols=near(signed, signed), smooth_rows=smooth_rows,
        fold_first=fold_first, fold_last=fold_last, total=float(np.sum(profile**2) ** 2),
    )


def dot(left, right):
    return jnp.dot(left, right, preferred_element_type=F32)


def parts_of(values):
    high = values.astype(BF16)
    return high, (values - high.astype(F32)).astype(BF16)


def fine_left(matrix, values):
    high, low = parts_of(values)
    return dot(matrix, high) + dot(matrix, low)


def fine_right(values, matrix):
    high, low = parts_of(values)
    return dot(high, matrix) + dot(low, matrix)


def contrast(number, planes):
    if number < 3:
        return planes[2 * number] - planes[2 * number + 1]
    pair = [planes[2 * i] + planes[2 * i + 1] for i in range(3)]
    if number == 3:
        return (pair[0] - pair[1]) * 0.5**0.5
    return (pair[0] + pair[1] - 2.0 * pair[2]) * (1.0 / 6.0) ** 0.5


WEIGHT = 0.5
PLANES = 5


def first_lane(rows, cols):
    return lax.broadcasted_iota(jnp.int32, (rows, cols), 1) == 0


def first_row(rows, cols):
    return lax.broadcasted_iota(jnp.int32, (rows, cols), 0) == 0


def edge_line(squares):
    half = squares.shape[1] // 2
    lane = first_lane(squares.shape[0], half)
    left, right = squares[:, :half], squares[:, half:]
    both = left + right
    return jnp.concatenate([jnp.where(lane, left, both), jnp.where(lane, right, both)], axis=1)


def mirrored_cols(values):
    half = values.shape[1] // 2
    lane = first_lane(values.shape[0], half)
    left, right = values[:, :half], values[:, half:]
    return jnp.concatenate([jnp.where(lane, left, right), jnp.where(lane, right, left)], axis=1)


def gains(power, edge_rows, edge_cols, smooth_rows, smooth_cols, fold_first, fold_last):
    half = power.shape[0]
    lane = first_lane(half, 128)
    whole = jnp.concatenate(
        [
            jnp.where(lane, edge_cols[:, :128], power[:, :128]), power[:, 128:half],
            jnp.where(lane, edge_cols[:, 128:], power[:, half : half + 128]), power[:, half + 128 :],
        ],
        axis=1,
    )
    top = jnp.where(first_row(8, 2 * half), edge_line(edge_rows[:8]), whole[:8])
    nyquist = edge_line(edge_rows[8:])
    whole = jnp.concatenate([top, whole[8:], nyquist, jnp.zeros_like(nyquist)], axis=0)
    once = fine_right(whole, smooth_cols)
    smooth = fine_left(smooth_rows, once[:half])
    start = smooth[:PAD] + fine_left(fold_first, mirrored_cols(once[:PAD]))
    tail = jnp.concatenate([mirrored_cols(once[half - PAD : half]), once[half:]], axis=0)
    end = smooth[half - PAD :] + fine_left(fold_last, tail)
    return jnp.sqrt(jnp.concatenate([start, smooth[PAD : half - PAD], end[: PAD + 8]], axis=0))


def combine(noise, factor, sums, edge, last):
    half = noise.shape[0] // 2
    values = noise * factor
    a, b = values[:half, :half], values[:half, half:]
    d, e = values[half:, :half], values[half:, half:]
    rows, lane = first_row(half, half), first_lane(half, half)
    either, both = rows | lane, rows & lane
    zero = jnp.zeros_like(a)
    sums[0] = jnp.where(both, a, 2.0 * (a - jnp.where(either, zero, e)))
    sums[1] = 2.0 * (jnp.where(lane, zero, b) + jnp.where(rows, zero, d))
    sums[2] = jnp.where(either, zero, 2.0 * (a + e))
    sums[3] = jnp.where(either, zero, 2.0 * (b - d))
    edge[0] = jnp.where(both, b, 2.0 * b)[:, :128]
    edge[1] = (2.0 * e)[:, :128]
    bottom = values[half : half + 8]
    single = first_lane(8, half)
    single = jnp.concatenate([single, single], axis=1)
    last[...] = jnp.where(single, bottom, 2.0 * bottom)


def shaped(gain, sums, edge, last):
    half = sums.shape[1]
    plus, minus = gain[:half, :half], gain[:half, half:]
    lane = first_lane(half, 128)
    row = first_row(8, half)
    line = gain[half : half + 8] * last[...]

    def with_lane(values, fixed):
        return jnp.concatenate([jnp.where(lane, minus[:, :128] * fixed, values[:, :128]), values[:, 128:]], axis=1)

    def with_row(values, fixed):
        return jnp.concatenate([jnp.where(row, fixed, values[:8]), values[8:]], axis=0)

    real_plus, imag_plus = plus * sums[0], plus * sums[1]
    real_minus, imag_minus = (minus * sums[2]).astype(BF16), (minus * sums[3]).astype(BF16)
    return (
        jnp.concatenate([real_plus.astype(BF16), with_lane(imag_plus, edge[0]).astype(BF16)], axis=1),
        jnp.concatenate(
            [
                with_row(imag_plus, line[:, :half]).astype(BF16),
                with_row(with_lane(-real_plus, edge[1]), line[:, half:]).astype(BF16),
            ],
            axis=1,
        ),
        jnp.concatenate([real_minus, imag_minus], axis=1),
        jnp.concatenate([-imag_minus, real_minus], axis=1),
    )


def kernel(
    n_dec, n_ra, factor,
    maps_hbm, noise_hbm, table_hbm, turned_hbm, rows_hbm, cols_hbm, first_hbm, last_hbm,
    tall_hbm, wide_hbm,
    out_ref,
    maps, noise, table, turned, smooth_rows, smooth_cols, fold_first, fold_last,
    tall_ref, wide_ref,
    ext, window, power, edge_rows, edge_cols, spectrum, sums, edge, last, real,
    strip_out, strip_in, row_out, row_in,
    local_sem, send_sem, recv_sem, fold_send, fold_recv,
):
    dec, ra = lax.axis_index("dec"), lax.axis_index("ra")
    length = noise.shape[0]
    core = length // 2
    margin = core // 2
    half = core
    low, mid, high = pl.ds(0, margin), pl.ds(margin, core), pl.ds(margin + core, margin)
    head, tail = pl.ds(margin, margin), pl.ds(core, margin)
    exists = {"up": dec > 0, "down": dec < n_dec - 1, "left": ra > 0, "right": ra < n_ra - 1}
    target = {
        "up": {"dec": dec - 1}, "down": {"dec": dec + 1},
        "left": {"ra": ra - 1}, "right": {"ra": ra + 1},
    }
    opposite = {"up": "down", "down": "up", "left": "right", "right": "left"}

    pairs = [
        pltpu.make_async_copy(maps_hbm.at[pl.ds(2 * i, 2)], maps.at[pl.ds(2 * i, 2)], local_sem.at[i])
        for i in range(3)
    ]
    loads = [
        pltpu.make_async_copy(source, place, local_sem.at[3 + number])
        for number, (source, place) in enumerate(
            [(tall_hbm, tall_ref), (wide_hbm, wide_ref), (noise_hbm, noise), (table_hbm, table),
             (turned_hbm, turned), (rows_hbm, smooth_rows), (cols_hbm, smooth_cols),
             (first_hbm, fold_first), (last_hbm, fold_last)]
        )
    ]
    for load in pairs:
        load.start()

    barrier = pltpu.get_barrier_semaphore()
    for way in exists:
        @pl.when(exists[way])
        def _(way=way):
            pl.semaphore_signal(barrier, inc=1, device_id=target[way], device_id_type=MESH)
    inner = pl.ds(1, 2)
    moves = [
        ("up", head, 1, high, 1), ("down", tail, 1, low, 1),
        ("up", head, 2, high, 2), ("down", tail, 2, low, 2),
        ("left", mid, 1, mid, 3), ("right", mid, 2, mid, 0),
        ("left", high, 1, high, 3), ("left", low, 1, low, 3),
        ("right", high, 2, high, 0), ("right", low, 2, low, 0),
    ]

    def move(plane, number):
        way, rows, blocks, to_rows, to_blocks = moves[number]
        return pltpu.make_async_remote_copy(
            src_ref=ext.at[plane, blocks, rows, :],
            dst_ref=ext.at[plane, to_blocks, to_rows, :],
            send_sem=send_sem.at[plane, number],
            recv_sem=recv_sem.at[plane, number],
            device_id=target[way],
            device_id_type=MESH,
        )

    def start(plane, numbers):
        for number in numbers:
            @pl.when(exists[moves[number][0]])
            def _(number=number):
                move(plane, number).start()

    def wait_recv(plane, numbers):
        for number in numbers:
            @pl.when(exists[opposite[moves[number][0]]])
            def _(number=number):
                move(plane, number).wait_recv()

    def wait_send(plane, numbers):
        for number in numbers:
            @pl.when(exists[moves[number][0]])
            def _(number=number):
                move(plane, number).wait_send()

    for plane in range(PLANES):
        if plane < 3:
            pairs[plane].wait()
        used = range(6) if plane >= 3 else range(2 * plane, 2 * plane + 2)
        values = contrast(plane, {s: maps[s].astype(F32) for s in used}).astype(BF16)
        ext[plane, 1, mid, :] = values[:, :margin]
        ext[plane, 2, mid, :] = values[:, margin:]
        if plane == 0:
            pl.semaphore_wait(barrier, sum(here.astype(jnp.int32) for here in exists.values()))
        start(plane, (0, 3, 2, 1, 4, 5))

    for load in loads:
        load.start()
    whole = pl.ds(0, length)
    for way, rows, blocks in (
        ("up", low, inner), ("down", high, inner), ("left", whole, pl.ds(0, 1)), ("right", whole, pl.ds(3, 1)),
    ):
        @pl.when(jnp.logical_not(exists[way]))
        def _(rows=rows, blocks=blocks):
            ext[:, blocks, rows, :] = jnp.zeros((PLANES, blocks.size, rows.size, margin), BF16)

    for load in loads:
        load.wait()
    window[...] = tall_ref[...] * wide_ref[...]
    for total in (power, edge_rows, edge_cols):
        total[...] = jnp.zeros_like(total)

    def transform(tile):
        return dot(dot(table[...], tile).astype(BF16), turned[...])

    combine(transform(noise[...]), factor, sums, edge, last)

    def forward_corners(plane):
        for number in (0, 3, 2, 1):
            wait_recv(plane, (number,))
            start(plane, (6 + number,))

    def windowed(plane, rows, blocks):
        tile = jnp.concatenate([ext[plane, block, rows, :] for block in blocks], axis=1)
        shape = jnp.concatenate(
            [window[rows, block * margin : (block + 1) * margin] for block in blocks], axis=1
        )
        return (shape * tile.astype(F32)).astype(BF16)

    def gather_power(plane):
        wait_recv(plane, range(4, 10))
        add_power(transform(windowed(plane, whole, range(4))))

    def outer_rows(values):
        return jnp.concatenate([values(low), values(high)], axis=0)

    def gather_last(plane):
        halves = dot(table[...], windowed(plane, whole, (1, 2))).astype(BF16)
        spectrum[...] = dot(halves, turned[mid, :])
        wait_recv(plane, (4, 5))
        sides = dot(table[:, mid], windowed(plane, mid, (0, 3)))
        wait_recv(plane, range(6, 10))
        corners = outer_rows(lambda rows: windowed(plane, rows, (0, 3)))
        outer_table = jnp.concatenate([table[:, low], table[:, high]], axis=1)
        sides = (sides + dot(outer_table, corners)).astype(BF16)
        add_power(spectrum[...] + dot(sides, outer_rows(lambda rows: turned[rows, :])))

    def add_power(values):
        a, b = values[:half, :half], values[:half, half:]
        d, e = values[half:, :half], values[half:, half:]
        square = lambda part: part * part
        power[:, :half] += square(a - e) + square(b + d)
        power[:, half:] += square(a + e) + square(b - d)
        edge_rows[:8] += square(values[:8])
        edge_rows[8:] += square(values[half : half + 8])
        edge_cols[:, :128] += square(a[:, :128]) + square(d[:, :128])
        edge_cols[:, 128:] += square(b[:, :128]) + square(e[:, :128])

    forward_corners(0)
    forward_corners(1)

    def step(plane, carry):
        forward_corners(plane)
        gather_power(plane - 2)
        return carry

    lax.fori_loop(2, PLANES, step, 0)
    gather_power(PLANES - 2)
    gather_last(PLANES - 1)

    gain = gains(
        power[...], edge_rows[...], edge_cols[...], smooth_rows[...], smooth_cols[...],
        fold_first[...], fold_last[...],
    )
    mixed = jnp.concatenate(shaped(gain, sums, edge, last), axis=0)

    def inverse(rows):
        return dot(jnp.concatenate([rows, rows], axis=1), mixed).astype(BF16)

    def synthesize(part, rows, cols):
        real[rows, cols] = window[rows, cols] * dot(part, table[:, cols])

    def strip(side, rows, number):
        return pltpu.make_async_remote_copy(
            src_ref=strip_out.at[side, rows, :],
            dst_ref=strip_in.at[side, rows, :],
            send_sem=fold_send.at[side, number],
            recv_sem=fold_recv.at[side, number],
            device_id=target[("left", "right")[side]],
            device_id_type=MESH,
        )

    def band(side):
        return pltpu.make_async_remote_copy(
            src_ref=row_out.at[side],
            dst_ref=row_in.at[side],
            send_sem=fold_send.at[side, 3],
            recv_sem=fold_recv.at[side, 3],
            device_id=target[("up", "down")[side]],
            device_id_type=MESH,
        )

    pieces = ((low, 0), (high, 1), (mid, 2))
    ways = ("left", "right")
    side_table = jnp.concatenate([table[:, low], table[:, high]], axis=1)

    def send_strips(part, numbers):
        values = dot(part, side_table)
        start = 0
        for number in numbers:
            rows = pieces[number][0]
            for side, cols in enumerate((low, high)):
                block = values[start : start + rows.size, side * margin : (side + 1) * margin]
                strip_out[side, rows, :] = (window[rows, cols] * block).astype(BF16)
                @pl.when(exists[ways[side]])
                def _(side=side, rows=rows, number=number):
                    strip(side, rows, number).start()
            start += rows.size

    outer = inverse(outer_rows(lambda rows: turned[rows, :]))
    send_strips(outer, (0, 1))
    middle = inverse(turned[mid, :])
    send_strips(middle, (2,))
    for part, (rows, number) in zip((outer[:margin], outer[margin:], middle), pieces):
        synthesize(part, rows, mid)

    def drain(plane, carry):
        wait_send(plane, range(10))
        return carry

    lax.fori_loop(0, PLANES, drain, 0)

    def fold_columns(rows, number):
        for side, cols in ((1, head), (0, tail)):
            @pl.when(exists[opposite[ways[side]]])
            def _(side=side, cols=cols):
                strip(side, rows, number).wait_recv()
                real[rows, cols] += strip_in[side, rows, :].astype(F32)

    for side, (rows, number) in enumerate(pieces[:2]):
        fold_columns(rows, number)
        row_out[side] = real[rows, mid].astype(BF16)
        @pl.when(exists[("up", "down")[side]])
        def _(side=side):
            band(side).start()
    fold_columns(*pieces[2])
    for side, rows in ((1, head), (0, tail)):
        @pl.when(exists[("down", "up")[side]])
        def _(side=side, rows=rows):
            band(side).wait_recv()
            real[rows, mid] += row_in[side].astype(F32)
    out_ref[...] = real[mid, mid]

    for side in range(2):
        @pl.when(exists[ways[side]])
        def _(side=side):
            for rows, number in pieces:
                strip(side, rows, number).wait_send()

        @pl.when(exists[("up", "down")[side]])
        def _(side=side):
            band(side).wait_send()


def shards(n_dec, n_ra, constants, split_maps, white_noise):
    splits, core = split_maps.shape[0], split_maps.shape[1]
    length, half, margin = 2 * core, core, core // 2
    as_bf16 = lambda values: jnp.asarray(np.asarray(values, np.float32).astype(jnp.bfloat16))
    as_f32 = lambda values: jnp.asarray(np.asarray(values, np.float32))
    packed = as_bf16(constants["packed"])
    turned = as_bf16(constants["packed"].T)
    scale = WEIGHT / ((splits - 1) * constants["total"] * (2 * SMOOTH + 1) ** 2)
    in_vmem = pl.BlockSpec(memory_space=pltpu.VMEM)
    in_hbm = pl.BlockSpec(memory_space=pl.ANY)
    result = pl.pallas_call(
        functools.partial(kernel, n_dec, n_ra, scale**0.5),
        out_shape=pltpu.VMEM((core, core), F32),
        in_specs=[in_hbm] * 10,
        out_specs=in_vmem,
        scratch_shapes=[
            pltpu.VMEM((splits, core, core), BF16),
            pltpu.VMEM((length, length), BF16),
            pltpu.VMEM((length, length), BF16),
            pltpu.VMEM((length, length), BF16),
            pltpu.VMEM((half + PAD, half), BF16),
            pltpu.VMEM((length, length), BF16),
            pltpu.VMEM((PAD, PAD), BF16),
            pltpu.VMEM((2 * PAD, 2 * PAD), BF16),
            pltpu.VMEM((length, 1), F32),
            pltpu.VMEM((1, length), F32),
            pltpu.VMEM((PLANES, 4, length, margin), BF16),
            pltpu.VMEM((length, length), F32),
            pltpu.VMEM((half, length), F32),
            pltpu.VMEM((PAD, length), F32),
            pltpu.VMEM((half, 256), F32),
            pltpu.VMEM((length, length), F32),
            pltpu.VMEM((4, half, half), F32),
            pltpu.VMEM((2, half, 128), F32),
            pltpu.VMEM((8, length), F32),
            pltpu.VMEM((length, length), F32),
            pltpu.VMEM((2, length, margin), BF16),
            pltpu.VMEM((2, length, margin), BF16),
            pltpu.VMEM((2, margin, core), BF16),
            pltpu.VMEM((2, margin, core), BF16),
            pltpu.SemaphoreType.DMA((13,)),
            pltpu.SemaphoreType.DMA((PLANES, 10)),
            pltpu.SemaphoreType.DMA((PLANES, 10)),
            pltpu.SemaphoreType.DMA((2, 4)),
            pltpu.SemaphoreType.DMA((2, 4)),
        ],
        compiler_params=pltpu.CompilerParams(
            collective_id=0, has_side_effects=True, vmem_limit_bytes=56 << 20
        ),
    )(
        split_maps, white_noise, packed, turned,
        as_bf16(constants["smooth_rows"]), as_bf16(constants["smooth_cols"]),
        as_bf16(constants["fold_first"]), as_bf16(constants["fold_last"]),
        as_f32(constants["profile"][:, None]), as_f32(constants["profile"][None, :]),
    )
    return result * (1.0 / (length * length))


def solution(mesh):
    n_dec, n_ra = mesh.shape["dec"], mesh.shape["ra"]

    def body(split_maps, white_noise):
        constants = make_constants(2 * split_maps.shape[1])
        return shards(n_dec, n_ra, constants, split_maps, white_noise)

    placed = (P(None, "dec", "ra"), P("dec", "ra"))
    return jax.shard_map(
        body, mesh=mesh, in_specs=placed, out_specs=P("dec", "ra"), check_vma=False
    )
```

```python
import functools

import jax
import jax.numpy as jnp
import numpy as np
from jax import lax
from jax.experimental import pallas as pl
from jax.experimental.pallas import tpu as pltpu
from jax.sharding import PartitionSpec as P

SMOOTH = 4
MESH = pl.DeviceIdType.MESH
F32 = jnp.float32
BF16 = jnp.bfloat16
PAD = 16


def make_constants(length):
    half = length // 2
    indices = np.arange(length)
    angles = (indices[:, None] * indices[None, :] % length) * (2.0 * np.pi / length)
    cos_table, sin_table = np.cos(angles), np.sin(angles)
    packed = np.concatenate([cos_table[: half + 1], sin_table[1:half]], axis=0)
    profile = np.sin(np.pi * (indices + 0.5) / length) ** 2

    def near(left, right):
        distance = np.abs(left[:, None] - right[None, :]) % length
        return (np.minimum(distance, length - distance) <= SMOOTH).astype(np.float64)

    signed = np.concatenate([np.arange(half + 1), -np.arange(1, half)])
    kept = np.arange(half + PAD)
    smooth_rows = near(kept, np.arange(half)) * (kept <= half)[:, None]
    first = np.arange(PAD)
    fold_first = near(first, -first) * (first > 0)[None, :]
    last = half - PAD + np.arange(2 * PAD)
    fold_last = np.zeros((2 * PAD, 2 * PAD))
    fold_last[:, :PAD] = near(last, -last[:PAD])
    fold_last[:, PAD] = near(last, np.array([half]))[:, 0]
    fold_last[last > half] = 0.0
    return dict(
        packed=packed, profile=profile, smooth_cols=near(signed, signed), smooth_rows=smooth_rows,
        fold_first=fold_first, fold_last=fold_last, total=float(np.sum(profile**2) ** 2),
    )


def dot(left, right):
    return jnp.dot(left, right, preferred_element_type=F32)


def parts_of(values):
    high = values.astype(BF16)
    return high, (values - high.astype(F32)).astype(BF16)


def fine_left(matrix, values):
    high, low = parts_of(values)
    return dot(matrix, high) + dot(matrix, low)


def fine_right(values, matrix):
    high, low = parts_of(values)
    return dot(high, matrix) + dot(low, matrix)


def contrast(number, planes):
    if number < 3:
        return planes[2 * number] - planes[2 * number + 1]
    pair = [planes[2 * i] + planes[2 * i + 1] for i in range(3)]
    if number == 3:
        return (pair[0] - pair[1]) * 0.5**0.5
    return (pair[0] + pair[1] - 2.0 * pair[2]) * (1.0 / 6.0) ** 0.5


WEIGHT = 0.5
PLANES = 5


def first_lane(rows, cols):
    return lax.broadcasted_iota(jnp.int32, (rows, cols), 1) == 0


def first_row(rows, cols):
    return lax.broadcasted_iota(jnp.int32, (rows, cols), 0) == 0


def edge_line(squares):
    half = squares.shape[1] // 2
    lane = first_lane(squares.shape[0], half)
    left, right = squares[:, :half], squares[:, half:]
    both = left + right
    return jnp.concatenate([jnp.where(lane, left, both), jnp.where(lane, right, both)], axis=1)


def mirrored_cols(values):
    half = values.shape[1] // 2
    lane = first_lane(values.shape[0], half)
    left, right = values[:, :half], values[:, half:]
    return jnp.concatenate([jnp.where(lane, left, right), jnp.where(lane, right, left)], axis=1)


def gains(power, edge_rows, edge_cols, smooth_rows, smooth_cols, fold_first, fold_last):
    half = power.shape[0]
    lane = first_lane(half, 128)
    whole = jnp.concatenate(
        [
            jnp.where(lane, edge_cols[:, :128], power[:, :128]), power[:, 128:half],
            jnp.where(lane, edge_cols[:, 128:], power[:, half : half + 128]), power[:, half + 128 :],
        ],
        axis=1,
    )
    top = jnp.where(first_row(8, 2 * half), edge_line(edge_rows[:8]), whole[:8])
    nyquist = edge_line(edge_rows[8:])
    whole = jnp.concatenate([top, whole[8:], nyquist, jnp.zeros_like(nyquist)], axis=0)
    once = fine_right(whole, smooth_cols)
    smooth = fine_left(smooth_rows, once[:half])
    start = smooth[:PAD] + fine_left(fold_first, mirrored_cols(once[:PAD]))
    tail = jnp.concatenate([mirrored_cols(once[half - PAD : half]), once[half:]], axis=0)
    end = smooth[half - PAD :] + fine_left(fold_last, tail)
    return jnp.sqrt(jnp.concatenate([start, smooth[PAD : half - PAD], end[: PAD + 8]], axis=0))


def combine(noise, factor, sums, edge, last):
    half = noise.shape[0] // 2
    values = noise * factor
    a, b = values[:half, :half], values[:half, half:]
    d, e = values[half:, :half], values[half:, half:]
    rows, lane = first_row(half, half), first_lane(half, half)
    either, both = rows | lane, rows & lane
    zero = jnp.zeros_like(a)
    sums[0] = jnp.where(both, a, 2.0 * (a - jnp.where(either, zero, e)))
    sums[1] = 2.0 * (jnp.where(lane, zero, b) + jnp.where(rows, zero, d))
    sums[2] = jnp.where(either, zero, 2.0 * (a + e))
    sums[3] = jnp.where(either, zero, 2.0 * (b - d))
    edge[0] = jnp.where(both, b, 2.0 * b)[:, :128]
    edge[1] = (2.0 * e)[:, :128]
    bottom = values[half : half + 8]
    single = first_lane(8, half)
    single = jnp.concatenate([single, single], axis=1)
    last[...] = jnp.where(single, bottom, 2.0 * bottom)


def shaped(gain, sums, edge, last):
    half = sums.shape[1]
    plus, minus = gain[:half, :half], gain[:half, half:]
    lane = first_lane(half, 128)
    row = first_row(8, half)
    line = gain[half : half + 8] * last[...]

    def with_lane(values, fixed):
        return jnp.concatenate([jnp.where(lane, minus[:, :128] * fixed, values[:, :128]), values[:, 128:]], axis=1)

    def with_row(values, fixed):
        return jnp.concatenate([jnp.where(row, fixed, values[:8]), values[8:]], axis=0)

    real_plus, imag_plus = plus * sums[0], plus * sums[1]
    real_minus, imag_minus = (minus * sums[2]).astype(BF16), (minus * sums[3]).astype(BF16)
    return (
        jnp.concatenate([real_plus.astype(BF16), with_lane(imag_plus, edge[0]).astype(BF16)], axis=1),
        jnp.concatenate(
            [
                with_row(imag_plus, line[:, :half]).astype(BF16),
                with_row(with_lane(-real_plus, edge[1]), line[:, half:]).astype(BF16),
            ],
            axis=1,
        ),
        jnp.concatenate([real_minus, imag_minus], axis=1),
        jnp.concatenate([-imag_minus, real_minus], axis=1),
    )


def kernel(
    n_dec, n_ra, factor,
    maps_hbm, noise_hbm, table_hbm, turned_hbm, rows_hbm, cols_hbm, first_hbm, last_hbm,
    tall_hbm, wide_hbm,
    out_ref,
    maps, noise, table, turned, smooth_rows, smooth_cols, fold_first, fold_last,
    tall_ref, wide_ref,
    ext, window, power, edge_rows, edge_cols, spectrum, sums, edge, last, real,
    strip_out, strip_in, row_out, row_in, corner_in,
    local_sem, send_sem, recv_sem, fold_send, fold_recv,
):
    dec, ra = lax.axis_index("dec"), lax.axis_index("ra")
    length = noise.shape[0]
    core = length // 2
    margin = core // 2
    half = core
    low, mid, high = pl.ds(0, margin), pl.ds(margin, core), pl.ds(margin + core, margin)
    head, tail = pl.ds(margin, margin), pl.ds(core, margin)
    exists = {"up": dec > 0, "down": dec < n_dec - 1, "left": ra > 0, "right": ra < n_ra - 1}
    target = {
        "up": {"dec": dec - 1}, "down": {"dec": dec + 1},
        "left": {"ra": ra - 1}, "right": {"ra": ra + 1},
    }
    opposite = {"up": "down", "down": "up", "left": "right", "right": "left"}

    pairs = [
        pltpu.make_async_copy(maps_hbm.at[pl.ds(2 * i, 2)], maps.at[pl.ds(2 * i, 2)], local_sem.at[i])
        for i in range(3)
    ]
    loads = [
        pltpu.make_async_copy(source, place, local_sem.at[3 + number])
        for number, (source, place) in enumerate(
            [(tall_hbm, tall_ref), (wide_hbm, wide_ref), (noise_hbm, noise), (table_hbm, table),
             (turned_hbm, turned), (rows_hbm, smooth_rows), (cols_hbm, smooth_cols),
             (first_hbm, fold_first), (last_hbm, fold_last)]
        )
    ]
    for load in pairs:
        load.start()

    barrier = pltpu.get_barrier_semaphore()
    for way in exists:
        @pl.when(exists[way])
        def _(way=way):
            pl.semaphore_signal(barrier, inc=1, device_id=target[way], device_id_type=MESH)
    inner = pl.ds(1, 2)
    moves = [
        ("up", head, 1, high, 1), ("down", tail, 1, low, 1),
        ("up", head, 2, high, 2), ("down", tail, 2, low, 2),
        ("left", mid, 1, mid, 3), ("right", mid, 2, mid, 0),
        ("left", high, 1, high, 3), ("left", low, 1, low, 3),
        ("right", high, 2, high, 0), ("right", low, 2, low, 0),
    ]

    def move(plane, number):
        way, rows, blocks, to_rows, to_blocks = moves[number]
        return pltpu.make_async_remote_copy(
            src_ref=ext.at[plane, blocks, rows, :],
            dst_ref=ext.at[plane, to_blocks, to_rows, :],
            send_sem=send_sem.at[plane, number],
            recv_sem=recv_sem.at[plane, number],
            device_id=target[way],
            device_id_type=MESH,
        )

    def start(plane, numbers):
        for number in numbers:
            @pl.when(exists[moves[number][0]])
            def _(number=number):
                move(plane, number).start()

    def wait_recv(plane, numbers):
        for number in numbers:
            @pl.when(exists[opposite[moves[number][0]]])
            def _(number=number):
                move(plane, number).wait_recv()

    def wait_send(plane, numbers):
        for number in numbers:
            @pl.when(exists[moves[number][0]])
            def _(number=number):
                move(plane, number).wait_send()

    for plane in range(PLANES):
        if plane < 3:
            pairs[plane].wait()
        used = range(6) if plane >= 3 else range(2 * plane, 2 * plane + 2)
        values = contrast(plane, {s: maps[s].astype(F32) for s in used}).astype(BF16)
        ext[plane, 1, mid, :] = values[:, :margin]
        ext[plane, 2, mid, :] = values[:, margin:]
        if plane == 0:
            pl.semaphore_wait(barrier, sum(here.astype(jnp.int32) for here in exists.values()))
        start(plane, (0, 3, 2, 1, 4, 5))

    for load in loads:
        load.start()
    whole = pl.ds(0, length)
    for way, rows, blocks in (
        ("up", low, inner), ("down", high, inner), ("left", whole, pl.ds(0, 1)), ("right", whole, pl.ds(3, 1)),
    ):
        @pl.when(jnp.logical_not(exists[way]))
        def _(rows=rows, blocks=blocks):
            ext[:, blocks, rows, :] = jnp.zeros((PLANES, blocks.size, rows.size, margin), BF16)

    for load in loads:
        load.wait()
    window[...] = tall_ref[...] * wide_ref[...]
    for total in (power, edge_rows, edge_cols):
        total[...] = jnp.zeros_like(total)

    def transform(tile):
        return dot(dot(table[...], tile).astype(BF16), turned[...])

    combine(transform(noise[...]), factor, sums, edge, last)

    def forward_corners(plane):
        for number in (0, 3, 2, 1):
            wait_recv(plane, (number,))
            start(plane, (6 + number,))

    def windowed(plane, rows, blocks):
        tile = jnp.concatenate([ext[plane, block, rows, :] for block in blocks], axis=1)
        shape = jnp.concatenate(
            [window[rows, block * margin : (block + 1) * margin] for block in blocks], axis=1
        )
        return (shape * tile.astype(F32)).astype(BF16)

    def gather_power(plane):
        wait_recv(plane, range(4, 10))
        add_power(transform(windowed(plane, whole, range(4))))

    def outer_rows(values):
        return jnp.concatenate([values(low), values(high)], axis=0)

    def gather_last(plane):
        halves = dot(table[...], windowed(plane, whole, (1, 2))).astype(BF16)
        spectrum[...] = dot(halves, turned[mid, :])
        wait_recv(plane, (4, 5))
        sides = dot(table[:, mid], windowed(plane, mid, (0, 3)))
        wait_recv(plane, range(6, 10))
        corners = outer_rows(lambda rows: windowed(plane, rows, (0, 3)))
        outer_table = jnp.concatenate([table[:, low], table[:, high]], axis=1)
        sides = (sides + dot(outer_table, corners)).astype(BF16)
        add_power(spectrum[...] + dot(sides, outer_rows(lambda rows: turned[rows, :])))

    def add_power(values):
        a, b = values[:half, :half], values[:half, half:]
        d, e = values[half:, :half], values[half:, half:]
        square = lambda part: part * part
        power[:, :half] += square(a - e) + square(b + d)
        power[:, half:] += square(a + e) + square(b - d)
        edge_rows[:8] += square(values[:8])
        edge_rows[8:] += square(values[half : half + 8])
        edge_cols[:, :128] += square(a[:, :128]) + square(d[:, :128])
        edge_cols[:, 128:] += square(b[:, :128]) + square(e[:, :128])

    forward_corners(0)
    forward_corners(1)

    def step(plane, carry):
        forward_corners(plane)
        gather_power(plane - 2)
        return carry

    lax.fori_loop(2, PLANES, step, 0)
    gather_power(PLANES - 2)
    gather_last(PLANES - 1)

    gain = gains(
        power[...], edge_rows[...], edge_cols[...], smooth_rows[...], smooth_cols[...],
        fold_first[...], fold_last[...],
    )
    mixed = jnp.concatenate(shaped(gain, sums, edge, last), axis=0)

    def inverse(rows):
        return dot(jnp.concatenate([rows, rows], axis=1), mixed).astype(BF16)

    def strip(side, rows, number):
        return pltpu.make_async_remote_copy(
            src_ref=strip_out.at[side, rows, :],
            dst_ref=strip_in.at[side, rows, :],
            send_sem=fold_send.at[side, number],
            recv_sem=fold_recv.at[side, number],
            device_id=target[("left", "right")[side]],
            device_id_type=MESH,
        )

    def band(side, part):
        return pltpu.make_async_remote_copy(
            src_ref=row_out.at[side, part],
            dst_ref=row_in.at[side, part],
            send_sem=fold_send.at[side, 3 + part],
            recv_sem=fold_recv.at[side, 3 + part],
            device_id=target[vertical[side]],
            device_id_type=MESH,
        )

    def corner(side):
        return pltpu.make_async_remote_copy(
            src_ref=strip_out.at[jnp.where(odd, 1, 0), (low, high)[side], :],
            dst_ref=corner_in.at[side],
            send_sem=fold_send.at[side, 5],
            recv_sem=fold_recv.at[side, 5],
            device_id={**target[("up", "down")[side]], "ra": jnp.where(odd, ra + 1, ra - 1)},
            device_id_type=MESH,
        )

    pieces = ((low, 0), (high, 1), (mid, 2))
    ways, vertical = ("left", "right"), ("up", "down")
    odd = ra % 2 == 1
    even = jnp.logical_not(odd)
    far = jnp.where(odd, exists["right"], exists["left"])

    def sends(side, number):
        return exists[ways[side]] & (True if number == 2 else (odd, even)[side])

    def receives(side, number):
        return exists[opposite[ways[side]]] & (True if number == 2 else (even, odd)[side])
    side_table = jnp.concatenate([table[:, low], table[:, high]], axis=1)
    first = jnp.where(odd, 1, 0)

    def put_strips(number, blocks):
        rows = pieces[number][0]
        for side, cols in enumerate((low, high)):
            strip_out[side, rows, :] = (window[rows, cols] * blocks[side]).astype(BF16)

            @pl.when(sends(side, number))
            def _(side=side):
                strip(side, rows, number).start()

    outer = inverse(outer_rows(lambda rows: turned[rows, :]))
    values = dot(outer, table[...])
    for number, (rows, _) in enumerate(pieces[:2]):
        block = values[number * margin : (number + 1) * margin]
        put_strips(number, (block[:, :margin], block[:, margin + core :]))

        @pl.when(exists[vertical[number]] & far)
        def _(number=number):
            corner(number).start()

        for part, cols in enumerate((head, tail)):
            inside = window[rows, cols] * block[:, margin * (1 + part) : margin * (2 + part)]
            real[rows, cols] = inside
            row_out[number, part] = inside.astype(BF16)

        @pl.when(exists[vertical[number]])
        def _(number=number):
            band(number, first).start()

    middle = inverse(turned[mid, :])
    values = dot(middle, side_table)
    put_strips(2, (values[:, :margin], values[:, margin:]))
    for number, (rows, _) in enumerate(pieces[:2]):
        for side, part, cols in ((1, 0, head), (0, 1, tail)):
            @pl.when(receives(side, number))
            def _(side=side, part=part, cols=cols, rows=rows, number=number):
                strip(side, rows, number).wait_recv()
                row_out[number, part] = (real[rows, cols] + strip_in[side, rows, :].astype(F32)).astype(BF16)

        @pl.when(exists[vertical[number]])
        def _(number=number):
            band(number, 1 - first).start()

    real[mid, mid] = window[mid, mid] * dot(middle, table[:, mid])

    def drain(plane, carry):
        wait_send(plane, range(10))
        return carry

    lax.fori_loop(0, PLANES, drain, 0)

    for side, cols in ((1, head), (0, tail)):
        @pl.when(receives(side, 2))
        def _(side=side, cols=cols):
            strip(side, mid, 2).wait_recv()
            real[mid, cols] += strip_in[side, mid, :].astype(F32)

    for side, rows in enumerate((tail, head)):
        @pl.when(exists[opposite[vertical[side]]] & far)
        def _(side=side):
            corner(side).wait_recv()

        for here, cols in ((even, head), (odd, tail)):
            @pl.when(exists[opposite[vertical[side]]] & far & here)
            def _(side=side, rows=rows, cols=cols):
                real[rows, cols] += corner_in[side].astype(F32)

    for side, rows in enumerate((tail, head)):
        @pl.when(exists[opposite[vertical[side]]])
        def _(side=side, rows=rows):
            for part in range(2):
                band(side, part).wait_recv()
            for part, cols in enumerate((head, tail)):
                real[rows, cols] += row_in[side, part].astype(F32)

    out_ref[...] = real[mid, mid]

    for side in range(2):
        for rows, number in pieces:
            @pl.when(sends(side, number))
            def _(side=side, rows=rows, number=number):
                strip(side, rows, number).wait_send()

        @pl.when(exists[vertical[side]])
        def _(side=side):
            for part in range(2):
                band(side, part).wait_send()

        @pl.when(exists[vertical[side]] & far)
        def _(side=side):
            corner(side).wait_send()


def shards(n_dec, n_ra, constants, split_maps, white_noise):
    splits, core = split_maps.shape[0], split_maps.shape[1]
    length, half, margin = 2 * core, core, core // 2
    as_bf16 = lambda values: jnp.asarray(np.asarray(values, np.float32).astype(jnp.bfloat16))
    as_f32 = lambda values: jnp.asarray(np.asarray(values, np.float32))
    packed = as_bf16(constants["packed"])
    turned = as_bf16(constants["packed"].T)
    scale = WEIGHT / ((splits - 1) * constants["total"] * (2 * SMOOTH + 1) ** 2)
    in_vmem = pl.BlockSpec(memory_space=pltpu.VMEM)
    in_hbm = pl.BlockSpec(memory_space=pl.ANY)
    result = pl.pallas_call(
        functools.partial(kernel, n_dec, n_ra, scale**0.5),
        out_shape=pltpu.VMEM((core, core), F32),
        in_specs=[in_hbm] * 10,
        out_specs=in_vmem,
        scratch_shapes=[
            pltpu.VMEM((splits, core, core), BF16),
            pltpu.VMEM((length, length), BF16),
            pltpu.VMEM((length, length), BF16),
            pltpu.VMEM((length, length), BF16),
            pltpu.VMEM((half + PAD, half), BF16),
            pltpu.VMEM((length, length), BF16),
            pltpu.VMEM((PAD, PAD), BF16),
            pltpu.VMEM((2 * PAD, 2 * PAD), BF16),
            pltpu.VMEM((length, 1), F32),
            pltpu.VMEM((1, length), F32),
            pltpu.VMEM((PLANES, 4, length, margin), BF16),
            pltpu.VMEM((length, length), F32),
            pltpu.VMEM((half, length), F32),
            pltpu.VMEM((PAD, length), F32),
            pltpu.VMEM((half, 256), F32),
            pltpu.VMEM((length, length), F32),
            pltpu.VMEM((4, half, half), F32),
            pltpu.VMEM((2, half, 128), F32),
            pltpu.VMEM((8, length), F32),
            pltpu.VMEM((length, length), F32),
            pltpu.VMEM((2, length, margin), BF16),
            pltpu.VMEM((2, length, margin), BF16),
            pltpu.VMEM((2, 2, margin, margin), BF16),
            pltpu.VMEM((2, 2, margin, margin), BF16),
            pltpu.VMEM((2, margin, margin), BF16),
            pltpu.SemaphoreType.DMA((13,)),
            pltpu.SemaphoreType.DMA((PLANES, 10)),
            pltpu.SemaphoreType.DMA((PLANES, 10)),
            pltpu.SemaphoreType.DMA((2, 6)),
            pltpu.SemaphoreType.DMA((2, 6)),
        ],
        compiler_params=pltpu.CompilerParams(
            collective_id=0, has_side_effects=True, vmem_limit_bytes=56 << 20
        ),
    )(
        split_maps, white_noise, packed, turned,
        as_bf16(constants["smooth_rows"]), as_bf16(constants["smooth_cols"]),
        as_bf16(constants["fold_first"]), as_bf16(constants["fold_last"]),
        as_f32(constants["profile"][:, None]), as_f32(constants["profile"][None, :]),
    )
    return result * (1.0 / (length * length))


def solution(mesh):
    n_dec, n_ra = mesh.shape["dec"], mesh.shape["ra"]

    def body(split_maps, white_noise):
        constants = make_constants(2 * split_maps.shape[1])
        return shards(n_dec, n_ra, constants, split_maps, white_noise)

    placed = (P(None, "dec", "ra"), P("dec", "ra"))
    return jax.shard_map(
        body, mesh=mesh, in_specs=placed, out_specs=P("dec", "ra"), check_vma=False
    )
```

```python
import functools

import jax
import jax.numpy as jnp
import numpy as np
from jax import lax
from jax.experimental import pallas as pl
from jax.experimental.pallas import tpu as pltpu
from jax.sharding import PartitionSpec as P

SMOOTH = 4
MESH = pl.DeviceIdType.MESH
F32 = jnp.float32
BF16 = jnp.bfloat16
PAD = 16


def make_constants(length):
    half = length // 2
    indices = np.arange(length)
    angles = (indices[:, None] * indices[None, :] % length) * (2.0 * np.pi / length)
    cos_table, sin_table = np.cos(angles), np.sin(angles)
    packed = np.concatenate([cos_table[: half + 1], sin_table[1:half]], axis=0)
    profile = np.sin(np.pi * (indices + 0.5) / length) ** 2

    def near(left, right):
        distance = np.abs(left[:, None] - right[None, :]) % length
        return (np.minimum(distance, length - distance) <= SMOOTH).astype(np.float64)

    signed = np.concatenate([np.arange(half + 1), -np.arange(1, half)])
    kept = np.arange(half + PAD)
    smooth_rows = near(kept, np.arange(half)) * (kept <= half)[:, None]
    first = np.arange(PAD)
    fold_first = near(first, -first) * (first > 0)[None, :]
    last = half - PAD + np.arange(2 * PAD)
    fold_last = np.zeros((2 * PAD, 2 * PAD))
    fold_last[:, :PAD] = near(last, -last[:PAD])
    fold_last[:, PAD] = near(last, np.array([half]))[:, 0]
    fold_last[last > half] = 0.0
    return dict(
        packed=packed, profile=profile, smooth_cols=near(signed, signed), smooth_rows=smooth_rows,
        fold_first=fold_first, fold_last=fold_last, total=float(np.sum(profile**2) ** 2),
    )


def dot(left, right):
    return jnp.dot(left, right, preferred_element_type=F32)


def parts_of(values):
    high = values.astype(BF16)
    return high, (values - high.astype(F32)).astype(BF16)


def fine_left(matrix, values):
    high, low = parts_of(values)
    return dot(matrix, high) + dot(matrix, low)


def fine_right(values, matrix):
    high, low = parts_of(values)
    return dot(high, matrix) + dot(low, matrix)


def contrast(number, planes):
    if number < 3:
        return planes[2 * number] - planes[2 * number + 1]
    pair = [planes[2 * i] + planes[2 * i + 1] for i in range(3)]
    if number == 3:
        return (pair[0] - pair[1]) * 0.5**0.5
    return (pair[0] + pair[1] - 2.0 * pair[2]) * (1.0 / 6.0) ** 0.5


WEIGHT = 0.5
PLANES = 5


def first_lane(rows, cols):
    return lax.broadcasted_iota(jnp.int32, (rows, cols), 1) == 0


def first_row(rows, cols):
    return lax.broadcasted_iota(jnp.int32, (rows, cols), 0) == 0


def edge_line(squares):
    half = squares.shape[1] // 2
    lane = first_lane(squares.shape[0], half)
    left, right = squares[:, :half], squares[:, half:]
    both = left + right
    return jnp.concatenate([jnp.where(lane, left, both), jnp.where(lane, right, both)], axis=1)


def mirrored_cols(values):
    half = values.shape[1] // 2
    lane = first_lane(values.shape[0], half)
    left, right = values[:, :half], values[:, half:]
    return jnp.concatenate([jnp.where(lane, left, right), jnp.where(lane, right, left)], axis=1)


def gains(power, edge_rows, edge_cols, smooth_rows, smooth_cols, fold_first, fold_last):
    half = power.shape[0]
    lane = first_lane(half, 128)
    whole = jnp.concatenate(
        [
            jnp.where(lane, edge_cols[:, :128], power[:, :128]), power[:, 128:half],
            jnp.where(lane, edge_cols[:, 128:], power[:, half : half + 128]), power[:, half + 128 :],
        ],
        axis=1,
    )
    top = jnp.where(first_row(8, 2 * half), edge_line(edge_rows[:8]), whole[:8])
    nyquist = edge_line(edge_rows[8:])
    whole = jnp.concatenate([top, whole[8:], nyquist, jnp.zeros_like(nyquist)], axis=0)
    once = fine_right(whole, smooth_cols)
    smooth = fine_left(smooth_rows, once[:half])
    start = smooth[:PAD] + fine_left(fold_first, mirrored_cols(once[:PAD]))
    tail = jnp.concatenate([mirrored_cols(once[half - PAD : half]), once[half:]], axis=0)
    end = smooth[half - PAD :] + fine_left(fold_last, tail)
    return jnp.sqrt(jnp.concatenate([start, smooth[PAD : half - PAD], end[: PAD + 8]], axis=0))


def combine(noise, factor, sums, edge, last):
    half = noise.shape[0] // 2
    values = noise * factor
    a, b = values[:half, :half], values[:half, half:]
    d, e = values[half:, :half], values[half:, half:]
    rows, lane = first_row(half, half), first_lane(half, half)
    either, both = rows | lane, rows & lane
    zero = jnp.zeros_like(a)
    sums[0] = jnp.where(both, a, 2.0 * (a - jnp.where(either, zero, e)))
    sums[1] = 2.0 * (jnp.where(lane, zero, b) + jnp.where(rows, zero, d))
    sums[2] = jnp.where(either, zero, 2.0 * (a + e))
    sums[3] = jnp.where(either, zero, 2.0 * (b - d))
    edge[0] = jnp.where(both, b, 2.0 * b)[:, :128]
    edge[1] = (2.0 * e)[:, :128]
    bottom = values[half : half + 8]
    single = first_lane(8, half)
    single = jnp.concatenate([single, single], axis=1)
    last[...] = jnp.where(single, bottom, 2.0 * bottom)


def shaped(gain, sums, edge, last):
    half = sums.shape[1]
    plus, minus = gain[:half, :half], gain[:half, half:]
    lane = first_lane(half, 128)
    row = first_row(8, half)
    line = gain[half : half + 8] * last[...]

    def with_lane(values, fixed):
        return jnp.concatenate([jnp.where(lane, minus[:, :128] * fixed, values[:, :128]), values[:, 128:]], axis=1)

    def with_row(values, fixed):
        return jnp.concatenate([jnp.where(row, fixed, values[:8]), values[8:]], axis=0)

    real_plus, imag_plus = plus * sums[0], plus * sums[1]
    real_minus, imag_minus = (minus * sums[2]).astype(BF16), (minus * sums[3]).astype(BF16)
    return (
        jnp.concatenate([real_plus.astype(BF16), with_lane(imag_plus, edge[0]).astype(BF16)], axis=1),
        jnp.concatenate(
            [
                with_row(imag_plus, line[:, :half]).astype(BF16),
                with_row(with_lane(-real_plus, edge[1]), line[:, half:]).astype(BF16),
            ],
            axis=1,
        ),
        jnp.concatenate([real_minus, imag_minus], axis=1),
        jnp.concatenate([-imag_minus, real_minus], axis=1),
    )


def kernel(
    n_dec, n_ra, factor,
    maps_hbm, noise_hbm, table_hbm, turned_hbm, rows_hbm, cols_hbm, first_hbm, last_hbm,
    tall_hbm, wide_hbm,
    out_ref,
    maps, noise, table, turned, smooth_rows, smooth_cols, fold_first, fold_last,
    tall_ref, wide_ref,
    ext, window, power, edge_rows, edge_cols, spectrum, sums, edge, last, real,
    strip_out, strip_in, row_out, row_in, corner_in,
    local_sem, send_sem, recv_sem, fold_send, fold_recv, diagonal_sem,
):
    dec, ra = lax.axis_index("dec"), lax.axis_index("ra")
    length = noise.shape[0]
    core = length // 2
    margin = core // 2
    half = core
    low, mid, high = pl.ds(0, margin), pl.ds(margin, core), pl.ds(margin + core, margin)
    head, tail = pl.ds(margin, margin), pl.ds(core, margin)
    exists = {"up": dec > 0, "down": dec < n_dec - 1, "left": ra > 0, "right": ra < n_ra - 1}
    target = {
        "up": {"dec": dec - 1}, "down": {"dec": dec + 1},
        "left": {"ra": ra - 1}, "right": {"ra": ra + 1},
    }
    opposite = {"up": "down", "down": "up", "left": "right", "right": "left"}
    odd = ra % 2 == 1
    even = jnp.logical_not(odd)
    first = jnp.where(odd, 1, 0)
    far = jnp.where(odd, exists["right"], exists["left"])
    across = {"ra": jnp.where(odd, ra + 1, ra - 1)}

    pairs = [
        pltpu.make_async_copy(maps_hbm.at[pl.ds(2 * i, 2)], maps.at[pl.ds(2 * i, 2)], local_sem.at[i])
        for i in range(3)
    ]
    loads = [
        pltpu.make_async_copy(source, place, local_sem.at[3 + number])
        for number, (source, place) in enumerate(
            [(tall_hbm, tall_ref), (wide_hbm, wide_ref), (noise_hbm, noise), (table_hbm, table),
             (turned_hbm, turned), (rows_hbm, smooth_rows), (cols_hbm, smooth_cols),
             (first_hbm, fold_first), (last_hbm, fold_last)]
        )
    ]
    for load in pairs:
        load.start()

    barrier = pltpu.get_barrier_semaphore()
    for way in exists:
        @pl.when(exists[way])
        def _(way=way):
            pl.semaphore_signal(barrier, inc=1, device_id=target[way], device_id_type=MESH)
    inner = pl.ds(1, 2)
    moves = [
        ("up", head, 1, high, 1), ("down", tail, 1, low, 1),
        ("up", head, 2, high, 2), ("down", tail, 2, low, 2),
        ("left", mid, 1, mid, 3), ("right", mid, 2, mid, 0),
        ("left", high, 1, high, 3), ("left", low, 1, low, 3),
        ("right", high, 2, high, 0), ("right", low, 2, low, 0),
    ]

    def move(plane, number):
        way, rows, blocks, to_rows, to_blocks = moves[number]
        return pltpu.make_async_remote_copy(
            src_ref=ext.at[plane, blocks, rows, :],
            dst_ref=ext.at[plane, to_blocks, to_rows, :],
            send_sem=send_sem.at[plane, number],
            recv_sem=recv_sem.at[plane, number],
            device_id=target[way],
            device_id_type=MESH,
        )

    vertical = ("up", "down")

    def leaves(plane, number):
        way = moves[number][0]
        if number < 6:
            return exists[way]
        return exists[way] & ((odd if way == "left" else even) | (plane < PLANES - 1))

    def arrives(plane, number):
        way = moves[number][0]
        if number < 6:
            return exists[opposite[way]]
        source = exists["down" if number % 2 == 0 else "up"]
        return exists[opposite[way]] & ((even if way == "left" else odd) | source | (plane < PLANES - 1))

    def diagonal(side):
        return pltpu.make_async_remote_copy(
            src_ref=ext.at[PLANES - 1, 1 + first, (head, tail)[side], :],
            dst_ref=ext.at[PLANES - 1, 3 - 3 * first, (high, low)[side], :],
            send_sem=diagonal_sem.at[side],
            recv_sem=recv_sem.at[PLANES - 1, 6 + 2 * first + side],
            device_id={**target[vertical[side]], **across},
            device_id_type=MESH,
        )

    def start(plane, numbers):
        for number in numbers:
            @pl.when(leaves(plane, number))
            def _(number=number):
                move(plane, number).start()

    def wait_recv(plane, numbers):
        for number in numbers:
            @pl.when(arrives(plane, number))
            def _(number=number):
                move(plane, number).wait_recv()

    def wait_send(plane, numbers):
        for number in numbers:
            @pl.when(leaves(plane, number))
            def _(number=number):
                move(plane, number).wait_send()

    for plane in range(PLANES):
        if plane < 3:
            pairs[plane].wait()
        used = range(6) if plane >= 3 else range(2 * plane, 2 * plane + 2)
        values = contrast(plane, {s: maps[s].astype(F32) for s in used}).astype(BF16)
        ext[plane, 1, mid, :] = values[:, :margin]
        ext[plane, 2, mid, :] = values[:, margin:]
        if plane == 0:
            pl.semaphore_wait(barrier, sum(here.astype(jnp.int32) for here in exists.values()))
        start(plane, (0, 3, 2, 1, 4, 5))

    for load in loads:
        load.start()
    whole = pl.ds(0, length)
    for way, rows, blocks in (
        ("up", low, inner), ("down", high, inner), ("left", whole, pl.ds(0, 1)), ("right", whole, pl.ds(3, 1)),
    ):
        @pl.when(jnp.logical_not(exists[way]))
        def _(rows=rows, blocks=blocks):
            ext[:, blocks, rows, :] = jnp.zeros((PLANES, blocks.size, rows.size, margin), BF16)

    for way, rows in (("up", low), ("down", high)):
        for here, block in ((even, 0), (odd, 3)):
            @pl.when(jnp.logical_not(exists[way]) & far & here)
            def _(rows=rows, block=block):
                ext[PLANES - 1, block, rows, :] = jnp.zeros((margin, margin), BF16)

    for load in loads:
        load.wait()
    window[...] = tall_ref[...] * wide_ref[...]
    for total in (power, edge_rows, edge_cols):
        total[...] = jnp.zeros_like(total)

    def transform(tile):
        return dot(dot(table[...], tile).astype(BF16), turned[...])

    combine(transform(noise[...]), factor, sums, edge, last)

    def forward_corners(plane):
        for number in (0, 3, 2, 1):
            wait_recv(plane, (number,))
            start(plane, (6 + number,))

    def windowed(plane, rows, blocks):
        tile = jnp.concatenate([ext[plane, block, rows, :] for block in blocks], axis=1)
        shape = jnp.concatenate(
            [window[rows, block * margin : (block + 1) * margin] for block in blocks], axis=1
        )
        return (shape * tile.astype(F32)).astype(BF16)

    def gather_power(plane):
        wait_recv(plane, range(4, 10))
        add_power(transform(windowed(plane, whole, range(4))))

    def outer_rows(values):
        return jnp.concatenate([values(low), values(high)], axis=0)

    def gather_last(plane):
        halves = dot(table[...], windowed(plane, whole, (1, 2))).astype(BF16)
        spectrum[...] = dot(halves, turned[mid, :])
        wait_recv(plane, (4, 5))
        sides = dot(table[:, mid], windowed(plane, mid, (0, 3)))
        wait_recv(plane, range(6, 10))
        corners = outer_rows(lambda rows: windowed(plane, rows, (0, 3)))
        outer_table = jnp.concatenate([table[:, low], table[:, high]], axis=1)
        sides = (sides + dot(outer_table, corners)).astype(BF16)
        add_power(spectrum[...] + dot(sides, outer_rows(lambda rows: turned[rows, :])))

    def add_power(values):
        a, b = values[:half, :half], values[:half, half:]
        d, e = values[half:, :half], values[half:, half:]
        square = lambda part: part * part
        power[:, :half] += square(a - e) + square(b + d)
        power[:, half:] += square(a + e) + square(b - d)
        edge_rows[:8] += square(values[:8])
        edge_rows[8:] += square(values[half : half + 8])
        edge_cols[:, :128] += square(a[:, :128]) + square(d[:, :128])
        edge_cols[:, 128:] += square(b[:, :128]) + square(e[:, :128])

    forward_corners(0)
    forward_corners(1)
    forward_corners(2)
    gather_power(0)
    for side in range(2):
        @pl.when(exists[vertical[side]] & far)
        def _(side=side):
            diagonal(side).start()

    forward_corners(3)

    def catch_up(plane, carry):
        gather_power(plane)
        return carry

    lax.fori_loop(1, 3, catch_up, 0)
    forward_corners(PLANES - 1)
    gather_power(PLANES - 2)
    gather_last(PLANES - 1)

    gain = gains(
        power[...], edge_rows[...], edge_cols[...], smooth_rows[...], smooth_cols[...],
        fold_first[...], fold_last[...],
    )
    mixed = jnp.concatenate(shaped(gain, sums, edge, last), axis=0)

    def inverse(rows):
        return dot(jnp.concatenate([rows, rows], axis=1), mixed).astype(BF16)

    def strip(side, rows, number):
        return pltpu.make_async_remote_copy(
            src_ref=strip_out.at[side, rows, :],
            dst_ref=strip_in.at[side, rows, :],
            send_sem=fold_send.at[side, number],
            recv_sem=fold_recv.at[side, number],
            device_id=target[("left", "right")[side]],
            device_id_type=MESH,
        )

    def band(side, part):
        return pltpu.make_async_remote_copy(
            src_ref=row_out.at[side, part],
            dst_ref=row_in.at[side, part],
            send_sem=fold_send.at[side, 3 + part],
            recv_sem=fold_recv.at[side, 3 + part],
            device_id=target[vertical[side]],
            device_id_type=MESH,
        )

    def corner(side):
        return pltpu.make_async_remote_copy(
            src_ref=strip_out.at[jnp.where(odd, 1, 0), (low, high)[side], :],
            dst_ref=corner_in.at[side],
            send_sem=fold_send.at[side, 5],
            recv_sem=fold_recv.at[side, 5],
            device_id={**target[vertical[side]], **across},
            device_id_type=MESH,
        )

    pieces = ((low, 0), (high, 1), (mid, 2))
    ways = ("left", "right")

    def sends(side, number):
        return exists[ways[side]] & (True if number == 2 else (odd, even)[side])

    def receives(side, number):
        return exists[opposite[ways[side]]] & (True if number == 2 else (even, odd)[side])
    side_table = jnp.concatenate([table[:, low], table[:, high]], axis=1)

    def put_strips(number, blocks):
        rows = pieces[number][0]
        for side, cols in enumerate((low, high)):
            strip_out[side, rows, :] = (window[rows, cols] * blocks[side]).astype(BF16)

            @pl.when(sends(side, number))
            def _(side=side):
                strip(side, rows, number).start()

    outer = inverse(outer_rows(lambda rows: turned[rows, :]))
    values = dot(outer, table[...])
    for number, (rows, _) in enumerate(pieces[:2]):
        block = values[number * margin : (number + 1) * margin]
        put_strips(number, (block[:, :margin], block[:, margin + core :]))

        @pl.when(exists[vertical[number]] & far)
        def _(number=number):
            corner(number).start()

        for part, cols in enumerate((head, tail)):
            inside = window[rows, cols] * block[:, margin * (1 + part) : margin * (2 + part)]
            real[rows, cols] = inside
            row_out[number, part] = inside.astype(BF16)

        @pl.when(exists[vertical[number]])
        def _(number=number):
            band(number, first).start()

    middle = inverse(turned[mid, :])
    values = dot(middle, side_table)
    put_strips(2, (values[:, :margin], values[:, margin:]))
    for number, (rows, _) in enumerate(pieces[:2]):
        for side, part, cols in ((1, 0, head), (0, 1, tail)):
            @pl.when(receives(side, number))
            def _(side=side, part=part, cols=cols, rows=rows, number=number):
                strip(side, rows, number).wait_recv()
                row_out[number, part] = (real[rows, cols] + strip_in[side, rows, :].astype(F32)).astype(BF16)

        @pl.when(exists[vertical[number]])
        def _(number=number):
            band(number, 1 - first).start()

    real[mid, mid] = window[mid, mid] * dot(middle, table[:, mid])

    def drain(plane, carry):
        wait_send(plane, range(10))
        return carry

    lax.fori_loop(0, PLANES, drain, 0)
    for side in range(2):
        @pl.when(exists[vertical[side]] & far)
        def _(side=side):
            diagonal(side).wait_send()


    for side, cols in ((1, head), (0, tail)):
        @pl.when(receives(side, 2))
        def _(side=side, cols=cols):
            strip(side, mid, 2).wait_recv()
            real[mid, cols] += strip_in[side, mid, :].astype(F32)

    for side, rows in enumerate((tail, head)):
        @pl.when(exists[opposite[vertical[side]]] & far)
        def _(side=side):
            corner(side).wait_recv()

        for here, cols in ((even, head), (odd, tail)):
            @pl.when(exists[opposite[vertical[side]]] & far & here)
            def _(side=side, rows=rows, cols=cols):
                real[rows, cols] += corner_in[side].astype(F32)

    for side, rows in enumerate((tail, head)):
        @pl.when(exists[opposite[vertical[side]]])
        def _(side=side, rows=rows):
            for part in range(2):
                band(side, part).wait_recv()
            for part, cols in enumerate((head, tail)):
                real[rows, cols] += row_in[side, part].astype(F32)

    out_ref[...] = real[mid, mid]

    for side in range(2):
        for rows, number in pieces:
            @pl.when(sends(side, number))
            def _(side=side, rows=rows, number=number):
                strip(side, rows, number).wait_send()

        @pl.when(exists[vertical[side]])
        def _(side=side):
            for part in range(2):
                band(side, part).wait_send()

        @pl.when(exists[vertical[side]] & far)
        def _(side=side):
            corner(side).wait_send()


def shards(n_dec, n_ra, constants, split_maps, white_noise):
    splits, core = split_maps.shape[0], split_maps.shape[1]
    length, half, margin = 2 * core, core, core // 2
    as_bf16 = lambda values: jnp.asarray(np.asarray(values, np.float32).astype(jnp.bfloat16))
    as_f32 = lambda values: jnp.asarray(np.asarray(values, np.float32))
    packed = as_bf16(constants["packed"])
    turned = as_bf16(constants["packed"].T)
    scale = WEIGHT / ((splits - 1) * constants["total"] * (2 * SMOOTH + 1) ** 2)
    in_vmem = pl.BlockSpec(memory_space=pltpu.VMEM)
    in_hbm = pl.BlockSpec(memory_space=pl.ANY)
    result = pl.pallas_call(
        functools.partial(kernel, n_dec, n_ra, scale**0.5),
        out_shape=pltpu.VMEM((core, core), F32),
        in_specs=[in_hbm] * 10,
        out_specs=in_vmem,
        scratch_shapes=[
            pltpu.VMEM((splits, core, core), BF16),
            pltpu.VMEM((length, length), BF16),
            pltpu.VMEM((length, length), BF16),
            pltpu.VMEM((length, length), BF16),
            pltpu.VMEM((half + PAD, half), BF16),
            pltpu.VMEM((length, length), BF16),
            pltpu.VMEM((PAD, PAD), BF16),
            pltpu.VMEM((2 * PAD, 2 * PAD), BF16),
            pltpu.VMEM((length, 1), F32),
            pltpu.VMEM((1, length), F32),
            pltpu.VMEM((PLANES, 4, length, margin), BF16),
            pltpu.VMEM((length, length), F32),
            pltpu.VMEM((half, length), F32),
            pltpu.VMEM((PAD, length), F32),
            pltpu.VMEM((half, 256), F32),
            pltpu.VMEM((length, length), F32),
            pltpu.VMEM((4, half, half), F32),
            pltpu.VMEM((2, half, 128), F32),
            pltpu.VMEM((8, length), F32),
            pltpu.VMEM((length, length), F32),
            pltpu.VMEM((2, length, margin), BF16),
            pltpu.VMEM((2, length, margin), BF16),
            pltpu.VMEM((2, 2, margin, margin), BF16),
            pltpu.VMEM((2, 2, margin, margin), BF16),
            pltpu.VMEM((2, margin, margin), BF16),
            pltpu.SemaphoreType.DMA((13,)),
            pltpu.SemaphoreType.DMA((PLANES, 10)),
            pltpu.SemaphoreType.DMA((PLANES, 10)),
            pltpu.SemaphoreType.DMA((2, 6)),
            pltpu.SemaphoreType.DMA((2, 6)),
            pltpu.SemaphoreType.DMA((2,)),
        ],
        compiler_params=pltpu.CompilerParams(
            collective_id=0, has_side_effects=True, vmem_limit_bytes=56 << 20
        ),
    )(
        split_maps, white_noise, packed, turned,
        as_bf16(constants["smooth_rows"]), as_bf16(constants["smooth_cols"]),
        as_bf16(constants["fold_first"]), as_bf16(constants["fold_last"]),
        as_f32(constants["profile"][:, None]), as_f32(constants["profile"][None, :]),
    )
    return result * (1.0 / (length * length))


def solution(mesh):
    n_dec, n_ra = mesh.shape["dec"], mesh.shape["ra"]

    def body(split_maps, white_noise):
        constants = make_constants(2 * split_maps.shape[1])
        return shards(n_dec, n_ra, constants, split_maps, white_noise)

    placed = (P(None, "dec", "ra"), P("dec", "ra"))
    return jax.shard_map(
        body, mesh=mesh, in_specs=placed, out_specs=P("dec", "ra"), check_vma=False
    )
```

```python
import functools

import jax
import jax.numpy as jnp
import numpy as np
from jax import lax
from jax.experimental import pallas as pl
from jax.experimental.pallas import tpu as pltpu
from jax.sharding import PartitionSpec as P

SMOOTH = 4
MESH = pl.DeviceIdType.MESH
F32 = jnp.float32
BF16 = jnp.bfloat16
PAD = 16


def make_constants(length):
    half = length // 2
    indices = np.arange(length)
    angles = (indices[:, None] * indices[None, :] % length) * (2.0 * np.pi / length)
    cos_table, sin_table = np.cos(angles), np.sin(angles)
    packed = np.concatenate([cos_table[: half + 1], sin_table[1:half]], axis=0)
    profile = np.sin(np.pi * (indices + 0.5) / length) ** 2

    def near(left, right):
        distance = np.abs(left[:, None] - right[None, :]) % length
        return (np.minimum(distance, length - distance) <= SMOOTH).astype(np.float64)

    parity = np.concatenate([np.arange(0, half, 2), np.arange(1, half, 2)])
    order = np.concatenate([parity, half + parity])
    signed = np.concatenate([np.arange(half + 1), -np.arange(1, half)])[order]
    kept = np.arange(half + PAD)
    smooth_rows = near(kept, np.arange(half)) * (kept <= half)[:, None]
    first = np.arange(PAD)
    fold_first = near(first, -first) * (first > 0)[None, :]
    last = half - PAD + np.arange(2 * PAD)
    fold_last = np.zeros((2 * PAD, 2 * PAD))
    fold_last[:, :PAD] = near(last, -last[:PAD])
    fold_last[:, PAD] = near(last, np.array([half]))[:, 0]
    fold_last[last > half] = 0.0
    return dict(
        packed=packed, packed_cols=packed[order], profile=profile, smooth_cols=near(signed, signed), smooth_rows=smooth_rows,
        fold_first=fold_first, fold_last=fold_last, total=float(np.sum(profile**2) ** 2),
    )


def dot(left, right):
    return jnp.dot(left, right, preferred_element_type=F32)


def parts_of(values):
    high = values.astype(BF16)
    return high, (values - high.astype(F32)).astype(BF16)


def fine_left(matrix, values):
    high, low = parts_of(values)
    return dot(matrix, high) + dot(matrix, low)


def fine_right(values, matrix):
    high, low = parts_of(values)
    return dot(high, matrix) + dot(low, matrix)


def contrast(number, planes):
    if number < 3:
        return planes[2 * number] - planes[2 * number + 1]
    pair = [planes[2 * i] + planes[2 * i + 1] for i in range(3)]
    if number == 3:
        return (pair[0] - pair[1]) * 0.5**0.5
    return (pair[0] + pair[1] - 2.0 * pair[2]) * (1.0 / 6.0) ** 0.5


WEIGHT = 0.5
PLANES = 5


def first_lane(rows, cols):
    return lax.broadcasted_iota(jnp.int32, (rows, cols), 1) == 0


def first_row(rows, cols):
    return lax.broadcasted_iota(jnp.int32, (rows, cols), 0) == 0


def edge_line(squares):
    half = squares.shape[1] // 2
    lane = first_lane(squares.shape[0], half)
    left, right = squares[:, :half], squares[:, half:]
    both = left + right
    return jnp.concatenate([jnp.where(lane, left, both), jnp.where(lane, right, both)], axis=1)


def mirrored_cols(values):
    half = values.shape[1] // 2
    lane = first_lane(values.shape[0], half)
    left, right = values[:, :half], values[:, half:]
    return jnp.concatenate([jnp.where(lane, left, right), jnp.where(lane, right, left)], axis=1)


def gains(power, edge_rows, edge_cols, smooth_rows, smooth_cols, fold_first, fold_last):
    half = power.shape[0]
    lane = first_lane(half, 128)
    whole = jnp.concatenate(
        [
            jnp.where(lane, edge_cols[:, :128], power[:, :128]), power[:, 128:half],
            jnp.where(lane, edge_cols[:, 128:], power[:, half : half + 128]), power[:, half + 128 :],
        ],
        axis=1,
    )
    top = jnp.where(first_row(8, 2 * half), edge_line(edge_rows[:8]), whole[:8])
    nyquist = edge_line(edge_rows[8:])
    whole = jnp.concatenate([top, whole[8:], nyquist, jnp.zeros_like(nyquist)], axis=0)
    once = fine_right(whole, smooth_cols)
    smooth = fine_left(smooth_rows, once[:half])
    start = smooth[:PAD] + fine_left(fold_first, mirrored_cols(once[:PAD]))
    tail = jnp.concatenate([mirrored_cols(once[half - PAD : half]), once[half:]], axis=0)
    end = smooth[half - PAD :] + fine_left(fold_last, tail)
    return jnp.sqrt(jnp.concatenate([start, smooth[PAD : half - PAD], end[: PAD + 8]], axis=0))


def combine(noise, factor, sums, edge, last):
    half = noise.shape[0] // 2
    values = noise * factor
    a, b = values[:half, :half], values[:half, half:]
    d, e = values[half:, :half], values[half:, half:]
    rows, lane = first_row(half, half), first_lane(half, half)
    either, both = rows | lane, rows & lane
    zero = jnp.zeros_like(a)
    sums[0] = jnp.where(both, a, 2.0 * (a - jnp.where(either, zero, e)))
    sums[1] = 2.0 * (jnp.where(lane, zero, b) + jnp.where(rows, zero, d))
    sums[2] = jnp.where(either, zero, 2.0 * (a + e))
    sums[3] = jnp.where(either, zero, 2.0 * (b - d))
    edge[0] = jnp.where(both, b, 2.0 * b)[:, :128]
    edge[1] = (2.0 * e)[:, :128]
    bottom = values[half : half + 8]
    single = first_lane(8, half)
    single = jnp.concatenate([single, single], axis=1)
    last[...] = jnp.where(single, bottom, 2.0 * bottom)


def shaped(gain, sums, edge, last):
    half = sums.shape[1]
    plus, minus = gain[:half, :half], gain[:half, half:]
    lane = first_lane(half, 128)
    row = first_row(8, half)
    line = gain[half : half + 8] * last[...]

    def with_lane(values, fixed):
        return jnp.concatenate([jnp.where(lane, minus[:, :128] * fixed, values[:, :128]), values[:, 128:]], axis=1)

    def with_row(values, fixed):
        return jnp.concatenate([jnp.where(row, fixed, values[:8]), values[8:]], axis=0)

    real_plus, imag_plus = plus * sums[0], plus * sums[1]
    real_minus, imag_minus = (minus * sums[2]).astype(BF16), (minus * sums[3]).astype(BF16)
    return (
        jnp.concatenate([real_plus.astype(BF16), with_lane(imag_plus, edge[0]).astype(BF16)], axis=1),
        jnp.concatenate(
            [
                with_row(imag_plus, line[:, :half]).astype(BF16),
                with_row(with_lane(-real_plus, edge[1]), line[:, half:]).astype(BF16),
            ],
            axis=1,
        ),
        jnp.concatenate([real_minus, imag_minus], axis=1),
        jnp.concatenate([-imag_minus, real_minus], axis=1),
    )


def kernel(
    n_dec, n_ra, factor,
    maps_hbm, noise_hbm, table_hbm, turned_hbm, table_cols_hbm, turned_cols_hbm, rows_hbm, cols_hbm, first_hbm, last_hbm,
    tall_hbm, wide_hbm,
    out_ref,
    maps, noise, table, turned, table_cols, turned_cols, smooth_rows, smooth_cols, fold_first, fold_last,
    tall_ref, wide_ref,
    ext, window, power, edge_rows, edge_cols, inner_part, outer_part, sums, edge, last, real,
    strip_out, strip_in, row_out, row_in, corner_in,
    local_sem, send_sem, recv_sem, fold_send, fold_recv, diagonal_sem,
):
    dec, ra = lax.axis_index("dec"), lax.axis_index("ra")
    length = noise.shape[0]
    core = length // 2
    margin = core // 2
    half = core
    low, mid, high = pl.ds(0, margin), pl.ds(margin, core), pl.ds(margin + core, margin)
    head, tail = pl.ds(margin, margin), pl.ds(core, margin)
    exists = {"up": dec > 0, "down": dec < n_dec - 1, "left": ra > 0, "right": ra < n_ra - 1}
    target = {
        "up": {"dec": dec - 1}, "down": {"dec": dec + 1},
        "left": {"ra": ra - 1}, "right": {"ra": ra + 1},
    }
    opposite = {"up": "down", "down": "up", "left": "right", "right": "left"}
    odd = ra % 2 == 1
    even = jnp.logical_not(odd)
    first = jnp.where(odd, 1, 0)
    far = jnp.where(odd, exists["right"], exists["left"])
    across = {"ra": jnp.where(odd, ra + 1, ra - 1)}

    pairs = [
        pltpu.make_async_copy(maps_hbm.at[pl.ds(2 * i, 2)], maps.at[pl.ds(2 * i, 2)], local_sem.at[i])
        for i in range(3)
    ]
    loads = [
        pltpu.make_async_copy(source, place, local_sem.at[3 + number])
        for number, (source, place) in enumerate(
            [(tall_hbm, tall_ref), (wide_hbm, wide_ref), (noise_hbm, noise), (table_hbm, table),
             (turned_cols_hbm, turned_cols), (turned_hbm, turned), (table_cols_hbm, table_cols),
             (rows_hbm, smooth_rows), (cols_hbm, smooth_cols), (first_hbm, fold_first), (last_hbm, fold_last)]
        )
    ]
    for load in pairs:
        load.start()

    barrier = pltpu.get_barrier_semaphore()
    for way in exists:
        @pl.when(exists[way])
        def _(way=way):
            pl.semaphore_signal(barrier, inc=1, device_id=target[way], device_id_type=MESH)
    inner = pl.ds(1, 2)
    moves = [
        ("up", head, 1, high, 1), ("down", tail, 1, low, 1),
        ("up", head, 2, high, 2), ("down", tail, 2, low, 2),
        ("left", mid, 1, mid, 3), ("right", mid, 2, mid, 0),
        ("left", high, 1, high, 3), ("left", low, 1, low, 3),
        ("right", high, 2, high, 0), ("right", low, 2, low, 0),
    ]

    def move(plane, number):
        way, rows, blocks, to_rows, to_blocks = moves[number]
        return pltpu.make_async_remote_copy(
            src_ref=ext.at[plane, blocks, rows, :],
            dst_ref=ext.at[plane, to_blocks, to_rows, :],
            send_sem=send_sem.at[plane, number],
            recv_sem=recv_sem.at[plane, number],
            device_id=target[way],
            device_id_type=MESH,
        )

    vertical = ("up", "down")

    def leaves(plane, number):
        way = moves[number][0]
        if number < 6:
            return exists[way]
        return exists[way] & ((odd if way == "left" else even) | (plane < PLANES - 1))

    def arrives(plane, number):
        way = moves[number][0]
        if number < 6:
            return exists[opposite[way]]
        source = exists["down" if number % 2 == 0 else "up"]
        return exists[opposite[way]] & ((even if way == "left" else odd) | source | (plane < PLANES - 1))

    def diagonal(side):
        return pltpu.make_async_remote_copy(
            src_ref=ext.at[PLANES - 1, 1 + first, (head, tail)[side], :],
            dst_ref=ext.at[PLANES - 1, 3 - 3 * first, (high, low)[side], :],
            send_sem=diagonal_sem.at[side],
            recv_sem=recv_sem.at[PLANES - 1, 6 + 2 * first + side],
            device_id={**target[vertical[side]], **across},
            device_id_type=MESH,
        )

    def start(plane, numbers):
        for number in numbers:
            @pl.when(leaves(plane, number))
            def _(number=number):
                move(plane, number).start()

    def wait_recv(plane, numbers):
        for number in numbers:
            @pl.when(arrives(plane, number))
            def _(number=number):
                move(plane, number).wait_recv()

    def wait_send(plane, numbers):
        for number in numbers:
            @pl.when(leaves(plane, number))
            def _(number=number):
                move(plane, number).wait_send()

    for plane in range(PLANES):
        if plane < 3:
            pairs[plane].wait()
        used = range(6) if plane >= 3 else range(2 * plane, 2 * plane + 2)
        values = contrast(plane, {s: maps[s].astype(F32) for s in used}).astype(BF16)
        ext[plane, 1, mid, :] = values[:, :margin]
        ext[plane, 2, mid, :] = values[:, margin:]
        if plane == 0:
            pl.semaphore_wait(barrier, sum(here.astype(jnp.int32) for here in exists.values()))
        start(plane, (0, 3, 2, 1, 4, 5))

    for load in loads:
        load.start()
    whole = pl.ds(0, length)
    for way, rows, blocks in (
        ("up", low, inner), ("down", high, inner), ("left", whole, pl.ds(0, 1)), ("right", whole, pl.ds(3, 1)),
    ):
        @pl.when(jnp.logical_not(exists[way]))
        def _(rows=rows, blocks=blocks):
            ext[:, blocks, rows, :] = jnp.zeros((PLANES, blocks.size, rows.size, margin), BF16)

    for way, rows in (("up", low), ("down", high)):
        for here, block in ((even, 0), (odd, 3)):
            @pl.when(jnp.logical_not(exists[way]) & far & here)
            def _(rows=rows, block=block):
                ext[PLANES - 1, block, rows, :] = jnp.zeros((margin, margin), BF16)

    for load in loads[:5]:
        load.wait()
    window[...] = tall_ref[...] * wide_ref[...]
    for total in (power, edge_rows, edge_cols):
        total[...] = jnp.zeros_like(total)

    combine(
        dot(dot(table[...], noise[...]).astype(BF16), turned_cols[...]), factor, sums, edge, last
    )

    def spectra(left, right):
        even_cols = jnp.concatenate([turned_cols[:half, :margin], turned_cols[:half, half : half + margin]], axis=1)
        odd_cols = jnp.concatenate([turned_cols[:half, margin:half], turned_cols[:half, half + margin :]], axis=1)
        evens = dot((left + right).astype(BF16), even_cols)
        odds = dot((left - right).astype(BF16), odd_cols)
        return jnp.concatenate([evens[:, :margin], odds[:, :margin], evens[:, margin:], odds[:, margin:]], axis=1)

    def forward_corners(plane):
        for number in (0, 3, 2, 1):
            wait_recv(plane, (number,))
            start(plane, (6 + number,))

    def windowed(plane, rows, blocks):
        tile = jnp.concatenate([ext[plane, block, rows, :] for block in blocks], axis=1)
        shape = jnp.concatenate(
            [window[rows, block * margin : (block + 1) * margin] for block in blocks], axis=1
        )
        return (shape * tile.astype(F32)).astype(BF16)

    def gather_power(plane):
        wait_recv(plane, range(4, 10))
        halves = dot(table[...], windowed(plane, whole, range(4)))
        add_power(spectra(halves[:, :half], halves[:, half:]))

    def outer_rows(values):
        return jnp.concatenate([values(low), values(high)], axis=0)

    def gather_inner(plane, slot):
        inner_part[slot] = dot(table[...], windowed(plane, whole, (1, 2)))
        wait_recv(plane, (4, 5))
        outer_part[slot] = dot(table[:, mid], windowed(plane, mid, (0, 3)))

    def gather_outer(plane, slot):
        wait_recv(plane, range(6, 10))
        corners = outer_rows(lambda rows: windowed(plane, rows, (0, 3)))
        outer_table = jnp.concatenate([table[:, low], table[:, high]], axis=1)
        sides = outer_part[slot] + dot(outer_table, corners)
        left = jnp.concatenate([sides[:, :margin], inner_part[slot, :, :margin]], axis=1)
        right = jnp.concatenate([inner_part[slot, :, margin:], sides[:, margin:]], axis=1)
        add_power(spectra(left, right))

    def add_power(values):
        a, b = values[:half, :half], values[:half, half:]
        d, e = values[half:, :half], values[half:, half:]
        square = lambda part: part * part
        power[:, :half] += square(a - e) + square(b + d)
        power[:, half:] += square(a + e) + square(b - d)
        edge_rows[:8] += square(values[:8])
        edge_rows[8:] += square(values[half : half + 8])
        edge_cols[:, :128] += square(a[:, :128]) + square(d[:, :128])
        edge_cols[:, 128:] += square(b[:, :128]) + square(e[:, :128])

    forward_corners(0)
    forward_corners(1)
    forward_corners(2)
    gather_power(0)
    for side in range(2):
        @pl.when(exists[vertical[side]] & far)
        def _(side=side):
            diagonal(side).start()

    forward_corners(3)

    def catch_up(plane, carry):
        gather_power(plane)
        return carry

    lax.fori_loop(1, 2, catch_up, 0)
    gather_inner(PLANES - 2, 0)
    forward_corners(PLANES - 1)
    gather_power(2)
    gather_inner(PLANES - 1, 1)
    for load in loads[5:]:
        load.wait()
    gather_outer(PLANES - 2, 0)
    gather_outer(PLANES - 1, 1)

    gain = gains(
        power[...], edge_rows[...], edge_cols[...], smooth_rows[...], smooth_cols[...],
        fold_first[...], fold_last[...],
    )
    mixed = jnp.concatenate(shaped(gain, sums, edge, last), axis=0)

    def inverse(rows):
        return dot(jnp.concatenate([rows, rows], axis=1), mixed).astype(BF16)

    def strip(side, rows, number):
        return pltpu.make_async_remote_copy(
            src_ref=strip_out.at[side, rows, :],
            dst_ref=strip_in.at[side, rows, :],
            send_sem=fold_send.at[side, number],
            recv_sem=fold_recv.at[side, number],
            device_id=target[("left", "right")[side]],
            device_id_type=MESH,
        )

    def band(side, part):
        return pltpu.make_async_remote_copy(
            src_ref=row_out.at[side, part],
            dst_ref=row_in.at[side, part],
            send_sem=fold_send.at[side, 3 + part],
            recv_sem=fold_recv.at[side, 3 + part],
            device_id=target[vertical[side]],
            device_id_type=MESH,
        )

    def corner(side):
        return pltpu.make_async_remote_copy(
            src_ref=strip_out.at[jnp.where(odd, 1, 0), (low, high)[side], :],
            dst_ref=corner_in.at[side],
            send_sem=fold_send.at[side, 5],
            recv_sem=fold_recv.at[side, 5],
            device_id={**target[vertical[side]], **across},
            device_id_type=MESH,
        )

    pieces = ((low, 0), (high, 1), (mid, 2))
    ways = ("left", "right")

    def sends(side, number):
        return exists[ways[side]] & (True if number == 2 else (odd, even)[side])

    def receives(side, number):
        return exists[opposite[ways[side]]] & (True if number == 2 else (even, odd)[side])
    side_table = jnp.concatenate([table_cols[:, low], table_cols[:, high]], axis=1)

    def put_strips(number, blocks):
        rows = pieces[number][0]
        for side, cols in enumerate((low, high)):
            strip_out[side, rows, :] = (window[rows, cols] * blocks[side]).astype(BF16)

            @pl.when(sends(side, number))
            def _(side=side):
                strip(side, rows, number).start()

    outer = inverse(outer_rows(lambda rows: turned[rows, :]))
    values = dot(outer, table_cols[...])
    for number, (rows, _) in enumerate(pieces[:2]):
        block = values[number * margin : (number + 1) * margin]
        put_strips(number, (block[:, :margin], block[:, margin + core :]))

        @pl.when(exists[vertical[number]] & far)
        def _(number=number):
            corner(number).start()

        for part, cols in enumerate((head, tail)):
            inside = window[rows, cols] * block[:, margin * (1 + part) : margin * (2 + part)]
            real[rows, cols] = inside
            row_out[number, part] = inside.astype(BF16)

        @pl.when(exists[vertical[number]])
        def _(number=number):
            band(number, first).start()

    middle = inverse(turned[mid, :])
    values = dot(middle, side_table)
    put_strips(2, (values[:, :margin], values[:, margin:]))
    for number, (rows, _) in enumerate(pieces[:2]):
        for side, part, cols in ((1, 0, head), (0, 1, tail)):
            @pl.when(receives(side, number))
            def _(side=side, part=part, cols=cols, rows=rows, number=number):
                strip(side, rows, number).wait_recv()
                row_out[number, part] = (real[rows, cols] + strip_in[side, rows, :].astype(F32)).astype(BF16)

        @pl.when(exists[vertical[number]])
        def _(number=number):
            band(number, 1 - first).start()

    real[mid, mid] = window[mid, mid] * dot(middle, table_cols[:, mid])

    def drain(plane, carry):
        wait_send(plane, range(10))
        return carry

    lax.fori_loop(0, PLANES, drain, 0)
    for side in range(2):
        @pl.when(exists[vertical[side]] & far)
        def _(side=side):
            diagonal(side).wait_send()


    for side, cols in ((1, head), (0, tail)):
        @pl.when(receives(side, 2))
        def _(side=side, cols=cols):
            strip(side, mid, 2).wait_recv()
            real[mid, cols] += strip_in[side, mid, :].astype(F32)

    for side, rows in enumerate((tail, head)):
        @pl.when(exists[opposite[vertical[side]]] & far)
        def _(side=side):
            corner(side).wait_recv()

        for here, cols in ((even, head), (odd, tail)):
            @pl.when(exists[opposite[vertical[side]]] & far & here)
            def _(side=side, rows=rows, cols=cols):
                real[rows, cols] += corner_in[side].astype(F32)

    for side, rows in enumerate((tail, head)):
        @pl.when(exists[opposite[vertical[side]]])
        def _(side=side, rows=rows):
            for part in range(2):
                band(side, part).wait_recv()
            for part, cols in enumerate((head, tail)):
                real[rows, cols] += row_in[side, part].astype(F32)

    out_ref[...] = real[mid, mid]

    for side in range(2):
        for rows, number in pieces:
            @pl.when(sends(side, number))
            def _(side=side, rows=rows, number=number):
                strip(side, rows, number).wait_send()

        @pl.when(exists[vertical[side]])
        def _(side=side):
            for part in range(2):
                band(side, part).wait_send()

        @pl.when(exists[vertical[side]] & far)
        def _(side=side):
            corner(side).wait_send()


def shards(n_dec, n_ra, constants, split_maps, white_noise):
    splits, core = split_maps.shape[0], split_maps.shape[1]
    length, half, margin = 2 * core, core, core // 2
    as_bf16 = lambda values: jnp.asarray(np.asarray(values, np.float32).astype(jnp.bfloat16))
    as_f32 = lambda values: jnp.asarray(np.asarray(values, np.float32))
    packed = as_bf16(constants["packed"])
    turned = as_bf16(constants["packed"].T)
    table_cols = as_bf16(constants["packed_cols"])
    turned_cols = as_bf16(constants["packed_cols"].T)
    scale = WEIGHT / ((splits - 1) * constants["total"] * (2 * SMOOTH + 1) ** 2)
    in_vmem = pl.BlockSpec(memory_space=pltpu.VMEM)
    in_hbm = pl.BlockSpec(memory_space=pl.ANY)
    result = pl.pallas_call(
        functools.partial(kernel, n_dec, n_ra, scale**0.5),
        out_shape=pltpu.VMEM((core, core), F32),
        in_specs=[in_hbm] * 12,
        out_specs=in_vmem,
        scratch_shapes=[
            pltpu.VMEM((splits, core, core), BF16),
            pltpu.VMEM((length, length), BF16),
            pltpu.VMEM((length, length), BF16),
            pltpu.VMEM((length, length), BF16),
            pltpu.VMEM((length, length), BF16),
            pltpu.VMEM((length, length), BF16),
            pltpu.VMEM((half + PAD, half), BF16),
            pltpu.VMEM((length, length), BF16),
            pltpu.VMEM((PAD, PAD), BF16),
            pltpu.VMEM((2 * PAD, 2 * PAD), BF16),
            pltpu.VMEM((length, 1), F32),
            pltpu.VMEM((1, length), F32),
            pltpu.VMEM((PLANES, 4, length, margin), BF16),
            pltpu.VMEM((length, length), F32),
            pltpu.VMEM((half, length), F32),
            pltpu.VMEM((PAD, length), F32),
            pltpu.VMEM((half, 256), F32),
            pltpu.VMEM((2, length, half), F32),
            pltpu.VMEM((2, length, half), F32),
            pltpu.VMEM((4, half, half), F32),
            pltpu.VMEM((2, half, 128), F32),
            pltpu.VMEM((8, length), F32),
            pltpu.VMEM((length, length), F32),
            pltpu.VMEM((2, length, margin), BF16),
            pltpu.VMEM((2, length, margin), BF16),
            pltpu.VMEM((2, 2, margin, margin), BF16),
            pltpu.VMEM((2, 2, margin, margin), BF16),
            pltpu.VMEM((2, margin, margin), BF16),
            pltpu.SemaphoreType.DMA((14,)),
            pltpu.SemaphoreType.DMA((PLANES, 10)),
            pltpu.SemaphoreType.DMA((PLANES, 10)),
            pltpu.SemaphoreType.DMA((2, 6)),
            pltpu.SemaphoreType.DMA((2, 6)),
            pltpu.SemaphoreType.DMA((2,)),
        ],
        compiler_params=pltpu.CompilerParams(
            collective_id=0, has_side_effects=True, vmem_limit_bytes=56 << 20
        ),
    )(
        split_maps, white_noise, packed, turned, table_cols, turned_cols,
        as_bf16(constants["smooth_rows"]), as_bf16(constants["smooth_cols"]),
        as_bf16(constants["fold_first"]), as_bf16(constants["fold_last"]),
        as_f32(constants["profile"][:, None]), as_f32(constants["profile"][None, :]),
    )
    return result * (1.0 / (length * length))


def solution(mesh):
    n_dec, n_ra = mesh.shape["dec"], mesh.shape["ra"]

    def body(split_maps, white_noise):
        constants = make_constants(2 * split_maps.shape[1])
        return shards(n_dec, n_ra, constants, split_maps, white_noise)

    placed = (P(None, "dec", "ra"), P("dec", "ra"))
    return jax.shard_map(
        body, mesh=mesh, in_specs=placed, out_specs=P("dec", "ra"), check_vma=False
    )
```

```python
import functools

import jax
import jax.numpy as jnp
import numpy as np
from jax import lax
from jax.experimental import pallas as pl
from jax.experimental.pallas import tpu as pltpu
from jax.sharding import PartitionSpec as P

SMOOTH = 4
MESH = pl.DeviceIdType.MESH
F32 = jnp.float32
BF16 = jnp.bfloat16
PAD = 16


def make_constants(length):
    half = length // 2
    indices = np.arange(length)
    angles = (indices[:, None] * indices[None, :] % length) * (2.0 * np.pi / length)
    cos_table, sin_table = np.cos(angles), np.sin(angles)
    packed = np.concatenate([cos_table[: half + 1], sin_table[1:half]], axis=0)
    profile = np.sin(np.pi * (indices + 0.5) / length) ** 2

    def near(left, right):
        distance = np.abs(left[:, None] - right[None, :]) % length
        return (np.minimum(distance, length - distance) <= SMOOTH).astype(np.float64)

    parity = np.concatenate([np.arange(0, half, 2), np.arange(1, half, 2)])
    order = np.concatenate([parity, half + parity])
    signed = np.concatenate([np.arange(half + 1), -np.arange(1, half)])[order]
    kept = np.arange(half + PAD)
    smooth_rows = near(kept, np.arange(half)) * (kept <= half)[:, None]
    first = np.arange(PAD)
    fold_first = near(first, -first) * (first > 0)[None, :]
    last = half - PAD + np.arange(2 * PAD)
    fold_last = np.zeros((2 * PAD, 2 * PAD))
    fold_last[:, :PAD] = near(last, -last[:PAD])
    fold_last[:, PAD] = near(last, np.array([half]))[:, 0]
    fold_last[last > half] = 0.0
    return dict(
        packed=packed, packed_cols=packed[order], profile=profile, smooth_cols=near(signed, signed), smooth_rows=smooth_rows,
        fold_first=fold_first, fold_last=fold_last, total=float(np.sum(profile**2) ** 2),
    )


def dot(left, right):
    return jnp.dot(left, right, preferred_element_type=F32)


def parts_of(values):
    high = values.astype(BF16)
    return high, (values - high.astype(F32)).astype(BF16)


def fine_left(matrix, values):
    high, low = parts_of(values)
    return dot(matrix, high) + dot(matrix, low)


def fine_right(values, matrix):
    high, low = parts_of(values)
    return dot(high, matrix) + dot(low, matrix)


def contrast(number, planes):
    if number < 3:
        return planes[2 * number] - planes[2 * number + 1]
    pair = [planes[2 * i] + planes[2 * i + 1] for i in range(3)]
    if number == 3:
        return (pair[0] - pair[1]) * 0.5**0.5
    return (pair[0] + pair[1] - 2.0 * pair[2]) * (1.0 / 6.0) ** 0.5


WEIGHT = 0.5
PLANES = 5


def first_lane(rows, cols):
    return lax.broadcasted_iota(jnp.int32, (rows, cols), 1) == 0


def first_row(rows, cols):
    return lax.broadcasted_iota(jnp.int32, (rows, cols), 0) == 0


def edge_line(squares):
    half = squares.shape[1] // 2
    lane = first_lane(squares.shape[0], half)
    left, right = squares[:, :half], squares[:, half:]
    both = left + right
    return jnp.concatenate([jnp.where(lane, left, both), jnp.where(lane, right, both)], axis=1)


def mirrored_cols(values):
    half = values.shape[1] // 2
    lane = first_lane(values.shape[0], half)
    left, right = values[:, :half], values[:, half:]
    return jnp.concatenate([jnp.where(lane, left, right), jnp.where(lane, right, left)], axis=1)


def gains(power, edge_rows, edge_cols, smooth_rows, smooth_cols, fold_first, fold_last):
    half = power.shape[0]
    lane = first_lane(half, 128)
    whole = jnp.concatenate(
        [
            jnp.where(lane, edge_cols[:, :128], power[:, :128]), power[:, 128:half],
            jnp.where(lane, edge_cols[:, 128:], power[:, half : half + 128]), power[:, half + 128 :],
        ],
        axis=1,
    )
    top = jnp.where(first_row(8, 2 * half), edge_line(edge_rows[:8]), whole[:8])
    nyquist = edge_line(edge_rows[8:])
    whole = jnp.concatenate([top, whole[8:], nyquist, jnp.zeros_like(nyquist)], axis=0)
    once = fine_right(whole, smooth_cols)
    smooth = fine_left(smooth_rows, once[:half])
    start = smooth[:PAD] + fine_left(fold_first, mirrored_cols(once[:PAD]))
    tail = jnp.concatenate([mirrored_cols(once[half - PAD : half]), once[half:]], axis=0)
    end = smooth[half - PAD :] + fine_left(fold_last, tail)
    return jnp.sqrt(jnp.concatenate([start, smooth[PAD : half - PAD], end[: PAD + 8]], axis=0))


def combine(noise, factor, sums, edge, last):
    half = noise.shape[0] // 2
    values = noise * factor
    a, b = values[:half, :half], values[:half, half:]
    d, e = values[half:, :half], values[half:, half:]
    rows, lane = first_row(half, half), first_lane(half, half)
    either, both = rows | lane, rows & lane
    zero = jnp.zeros_like(a)
    sums[0] = jnp.where(both, a, 2.0 * (a - jnp.where(either, zero, e)))
    sums[1] = 2.0 * (jnp.where(lane, zero, b) + jnp.where(rows, zero, d))
    sums[2] = jnp.where(either, zero, 2.0 * (a + e))
    sums[3] = jnp.where(either, zero, 2.0 * (b - d))
    edge[0] = jnp.where(both, b, 2.0 * b)[:, :128]
    edge[1] = (2.0 * e)[:, :128]
    bottom = values[half : half + 8]
    single = first_lane(8, half)
    single = jnp.concatenate([single, single], axis=1)
    last[...] = jnp.where(single, bottom, 2.0 * bottom)


def shaped(gain, sums, edge, last):
    half = sums.shape[1]
    plus, minus = gain[:half, :half], gain[:half, half:]
    lane = first_lane(half, 128)
    row = first_row(8, half)
    line = gain[half : half + 8] * last[...]

    def with_lane(values, fixed):
        return jnp.concatenate([jnp.where(lane, minus[:, :128] * fixed, values[:, :128]), values[:, 128:]], axis=1)

    def with_row(values, fixed):
        return jnp.concatenate([jnp.where(row, fixed, values[:8]), values[8:]], axis=0)

    real_plus, imag_plus = plus * sums[0], plus * sums[1]
    real_minus, imag_minus = (minus * sums[2]).astype(BF16), (minus * sums[3]).astype(BF16)
    return (
        jnp.concatenate([real_plus.astype(BF16), with_lane(imag_plus, edge[0]).astype(BF16)], axis=1),
        jnp.concatenate(
            [
                with_row(imag_plus, line[:, :half]).astype(BF16),
                with_row(with_lane(-real_plus, edge[1]), line[:, half:]).astype(BF16),
            ],
            axis=1,
        ),
        jnp.concatenate([real_minus, imag_minus], axis=1),
        jnp.concatenate([-imag_minus, real_minus], axis=1),
    )


def kernel(
    n_dec, n_ra, factor,
    maps_hbm, noise_hbm, table_hbm, turned_hbm, table_cols_hbm, turned_cols_hbm, rows_hbm, cols_hbm, first_hbm, last_hbm,
    tall_hbm, wide_hbm,
    out_ref,
    maps, noise, table, turned, table_cols, turned_cols, smooth_rows, smooth_cols, fold_first, fold_last,
    tall_ref, wide_ref,
    ext, window, power, edge_rows, edge_cols, inner_part, outer_part, sums, edge, last, real,
    strip_out, strip_in, row_out, row_in, corner_in,
    local_sem, send_sem, recv_sem, fold_send, fold_recv, diagonal_sem,
):
    dec, ra = lax.axis_index("dec"), lax.axis_index("ra")
    length = noise.shape[0]
    core = length // 2
    margin = core // 2
    half = core
    low, mid, high = pl.ds(0, margin), pl.ds(margin, core), pl.ds(margin + core, margin)
    head, tail = pl.ds(margin, margin), pl.ds(core, margin)
    exists = {"up": dec > 0, "down": dec < n_dec - 1, "left": ra > 0, "right": ra < n_ra - 1}
    target = {
        "up": {"dec": dec - 1}, "down": {"dec": dec + 1},
        "left": {"ra": ra - 1}, "right": {"ra": ra + 1},
    }
    opposite = {"up": "down", "down": "up", "left": "right", "right": "left"}
    odd = ra % 2 == 1
    even = jnp.logical_not(odd)
    first = jnp.where(odd, 1, 0)
    far = jnp.where(odd, exists["right"], exists["left"])
    across = {"ra": jnp.where(odd, ra + 1, ra - 1)}

    pairs = [
        pltpu.make_async_copy(maps_hbm.at[pl.ds(2 * i, 2)], maps.at[pl.ds(2 * i, 2)], local_sem.at[i])
        for i in range(3)
    ]
    loads = [
        pltpu.make_async_copy(source, place, local_sem.at[3 + number])
        for number, (source, place) in enumerate(
            [(tall_hbm, tall_ref), (wide_hbm, wide_ref), (noise_hbm, noise), (table_hbm, table),
             (turned_cols_hbm, turned_cols), (turned_hbm, turned), (table_cols_hbm, table_cols),
             (rows_hbm, smooth_rows), (cols_hbm, smooth_cols), (first_hbm, fold_first), (last_hbm, fold_last)]
        )
    ]
    for load in pairs:
        load.start()

    barrier = pltpu.get_barrier_semaphore()
    for way in exists:
        @pl.when(exists[way])
        def _(way=way):
            pl.semaphore_signal(barrier, inc=1, device_id=target[way], device_id_type=MESH)
    inner = pl.ds(1, 2)
    moves = [
        ("up", head, 1, high, 1), ("down", tail, 1, low, 1),
        ("up", head, 2, high, 2), ("down", tail, 2, low, 2),
        ("left", mid, 1, mid, 3), ("right", mid, 2, mid, 0),
        ("left", high, 1, high, 3), ("left", low, 1, low, 3),
        ("right", high, 2, high, 0), ("right", low, 2, low, 0),
    ]

    def move(plane, number):
        way, rows, blocks, to_rows, to_blocks = moves[number]
        return pltpu.make_async_remote_copy(
            src_ref=ext.at[plane, blocks, rows, :],
            dst_ref=ext.at[plane, to_blocks, to_rows, :],
            send_sem=send_sem.at[plane, number],
            recv_sem=recv_sem.at[plane, number],
            device_id=target[way],
            device_id_type=MESH,
        )

    vertical = ("up", "down")

    def leaves(plane, number):
        way = moves[number][0]
        if number < 6:
            return exists[way]
        return exists[way] & ((odd if way == "left" else even) | (plane < PLANES - 1))

    def arrives(plane, number):
        way = moves[number][0]
        if number < 6:
            return exists[opposite[way]]
        source = exists["down" if number % 2 == 0 else "up"]
        return exists[opposite[way]] & ((even if way == "left" else odd) | source | (plane < PLANES - 1))

    def diagonal(side):
        return pltpu.make_async_remote_copy(
            src_ref=ext.at[PLANES - 1, 1 + first, (head, tail)[side], :],
            dst_ref=ext.at[PLANES - 1, 3 - 3 * first, (high, low)[side], :],
            send_sem=diagonal_sem.at[side],
            recv_sem=recv_sem.at[PLANES - 1, 6 + 2 * first + side],
            device_id={**target[vertical[side]], **across},
            device_id_type=MESH,
        )

    def start(plane, numbers):
        for number in numbers:
            @pl.when(leaves(plane, number))
            def _(number=number):
                move(plane, number).start()

    def wait_recv(plane, numbers):
        for number in numbers:
            @pl.when(arrives(plane, number))
            def _(number=number):
                move(plane, number).wait_recv()

    def wait_send(plane, numbers):
        for number in numbers:
            @pl.when(leaves(plane, number))
            def _(number=number):
                move(plane, number).wait_send()

    for plane in range(PLANES):
        if plane < 3:
            pairs[plane].wait()
        used = range(6) if plane >= 3 else range(2 * plane, 2 * plane + 2)
        values = contrast(plane, {s: maps[s].astype(F32) for s in used}).astype(BF16)
        ext[plane, 1, mid, :] = values[:, :margin]
        ext[plane, 2, mid, :] = values[:, margin:]
        if plane == 0:
            pl.semaphore_wait(barrier, sum(here.astype(jnp.int32) for here in exists.values()))
        start(plane, (0, 3, 2, 1, 4, 5))

    for load in loads:
        load.start()
    whole = pl.ds(0, length)
    for way, rows, blocks in (
        ("up", low, inner), ("down", high, inner), ("left", whole, pl.ds(0, 1)), ("right", whole, pl.ds(3, 1)),
    ):
        @pl.when(jnp.logical_not(exists[way]))
        def _(rows=rows, blocks=blocks):
            ext[:, blocks, rows, :] = jnp.zeros((PLANES, blocks.size, rows.size, margin), BF16)

    for way, rows in (("up", low), ("down", high)):
        for here, block in ((even, 0), (odd, 3)):
            @pl.when(jnp.logical_not(exists[way]) & far & here)
            def _(rows=rows, block=block):
                ext[PLANES - 1, block, rows, :] = jnp.zeros((margin, margin), BF16)

    for load in loads[:5]:
        load.wait()
    window[...] = tall_ref[...] * wide_ref[...]
    for total in (power, edge_rows, edge_cols):
        total[...] = jnp.zeros_like(total)

    combine(
        dot(dot(table[...], noise[...]).astype(BF16), turned_cols[...]), factor, sums, edge, last
    )

    def spectra(left, right):
        even_cols = jnp.concatenate([turned_cols[:half, :margin], turned_cols[:half, half : half + margin]], axis=1)
        odd_cols = jnp.concatenate([turned_cols[:half, margin:half], turned_cols[:half, half + margin :]], axis=1)
        evens = dot((left + right).astype(BF16), even_cols)
        odds = dot((left - right).astype(BF16), odd_cols)
        return jnp.concatenate([evens[:, :margin], odds[:, :margin], evens[:, margin:], odds[:, margin:]], axis=1)

    def forward_corners(plane):
        for number in (0, 3, 2, 1):
            wait_recv(plane, (number,))
            start(plane, (6 + number,))

    def windowed(plane, rows, blocks):
        tile = jnp.concatenate([ext[plane, block, rows, :] for block in blocks], axis=1)
        shape = jnp.concatenate(
            [window[rows, block * margin : (block + 1) * margin] for block in blocks], axis=1
        )
        return (shape * tile.astype(F32)).astype(BF16)

    def gather_power(plane):
        wait_recv(plane, range(4, 10))
        halves = dot(table[...], windowed(plane, whole, range(4)))
        add_power(spectra(halves[:, :half], halves[:, half:]))

    def outer_rows(values):
        return jnp.concatenate([values(low), values(high)], axis=0)

    def gather_inner(plane, slot):
        inner_part[slot] = dot(table[...], windowed(plane, whole, (1, 2)))
        wait_recv(plane, (4, 5))
        outer_part[slot] = dot(table[:, mid], windowed(plane, mid, (0, 3)))

    def gather_outer(plane, slot):
        wait_recv(plane, range(6, 10))
        corners = outer_rows(lambda rows: windowed(plane, rows, (0, 3)))
        outer_table = jnp.concatenate([table[:, low], table[:, high]], axis=1)
        sides = outer_part[slot] + dot(outer_table, corners)
        left = jnp.concatenate([sides[:, :margin], inner_part[slot, :, :margin]], axis=1)
        right = jnp.concatenate([inner_part[slot, :, margin:], sides[:, margin:]], axis=1)
        add_power(spectra(left, right))

    def add_power(values):
        a, b = values[:half, :half], values[:half, half:]
        d, e = values[half:, :half], values[half:, half:]
        square = lambda part: part * part
        power[:, :half] += square(a - e) + square(b + d)
        power[:, half:] += square(a + e) + square(b - d)
        edge_rows[:8] += square(values[:8])
        edge_rows[8:] += square(values[half : half + 8])
        edge_cols[:, :128] += square(a[:, :128]) + square(d[:, :128])
        edge_cols[:, 128:] += square(b[:, :128]) + square(e[:, :128])

    forward_corners(0)
    forward_corners(1)
    forward_corners(2)
    gather_power(0)
    for side in range(2):
        @pl.when(exists[vertical[side]] & far)
        def _(side=side):
            diagonal(side).start()

    forward_corners(3)

    def catch_up(plane, carry):
        gather_power(plane)
        return carry

    lax.fori_loop(1, 2, catch_up, 0)
    gather_inner(PLANES - 2, 0)
    forward_corners(PLANES - 1)
    gather_power(2)
    gather_inner(PLANES - 1, 1)
    for load in loads[5:]:
        load.wait()
    gather_outer(PLANES - 2, 0)
    gather_outer(PLANES - 1, 1)

    gain = gains(
        power[...], edge_rows[...], edge_cols[...], smooth_rows[...], smooth_cols[...],
        fold_first[...], fold_last[...],
    )
    mixed = jnp.concatenate(shaped(gain, sums, edge, last), axis=0)

    def inverse(rows):
        return dot(jnp.concatenate([rows, rows], axis=1), mixed).astype(BF16)

    def strip(side, rows, number):
        return pltpu.make_async_remote_copy(
            src_ref=strip_out.at[side, rows, :],
            dst_ref=strip_in.at[side, rows, :],
            send_sem=fold_send.at[side, number],
            recv_sem=fold_recv.at[side, number],
            device_id=target[("left", "right")[side]],
            device_id_type=MESH,
        )

    def band(side, part):
        return pltpu.make_async_remote_copy(
            src_ref=row_out.at[side, part],
            dst_ref=row_in.at[side, part],
            send_sem=fold_send.at[side, 3 + part],
            recv_sem=fold_recv.at[side, 3 + part],
            device_id=target[vertical[side]],
            device_id_type=MESH,
        )

    def corner(side):
        return pltpu.make_async_remote_copy(
            src_ref=strip_out.at[jnp.where(odd, 1, 0), (low, high)[side], :],
            dst_ref=corner_in.at[side],
            send_sem=fold_send.at[side, 5],
            recv_sem=fold_recv.at[side, 5],
            device_id={**target[vertical[side]], **across},
            device_id_type=MESH,
        )

    pieces = ((low, 0), (high, 1), (mid, 2))
    ways = ("left", "right")

    def sends(side, number):
        return exists[ways[side]] & (True if number == 2 else (odd, even)[side])

    def receives(side, number):
        return exists[opposite[ways[side]]] & (True if number == 2 else (even, odd)[side])
    side_table = jnp.concatenate([table_cols[:, low], table_cols[:, high]], axis=1)

    def put_strips(number, blocks):
        rows = pieces[number][0]
        for side, cols in enumerate((low, high)):
            strip_out[side, rows, :] = (window[rows, cols] * blocks[side]).astype(BF16)

            @pl.when(sends(side, number))
            def _(side=side):
                strip(side, rows, number).start()

    outer = inverse(outer_rows(lambda rows: turned[rows, :]))
    values = dot(outer, table_cols[...])
    for number, (rows, _) in enumerate(pieces[:2]):
        block = values[number * margin : (number + 1) * margin]
        put_strips(number, (block[:, :margin], block[:, margin + core :]))

        @pl.when(exists[vertical[number]] & far)
        def _(number=number):
            corner(number).start()

        for part, cols in enumerate((head, tail)):
            inside = window[rows, cols] * block[:, margin * (1 + part) : margin * (2 + part)]
            real[rows, cols] = inside
            row_out[number, part] = inside.astype(BF16)

        @pl.when(exists[vertical[number]])
        def _(number=number):
            band(number, first).start()

    for number, (rows, _) in enumerate(pieces[:2]):
        for side, part, cols in ((1, 0, head), (0, 1, tail)):
            @pl.when(receives(side, number))
            def _(side=side, part=part, cols=cols, rows=rows, number=number):
                strip(side, rows, number).wait_recv()
                row_out[number, part] = (real[rows, cols] + strip_in[side, rows, :].astype(F32)).astype(BF16)

        @pl.when(exists[vertical[number]])
        def _(number=number):
            band(number, 1 - first).start()

    middle = inverse(turned[mid, :])
    values = dot(middle, side_table)
    put_strips(2, (values[:, :margin], values[:, margin:]))
    real[mid, mid] = window[mid, mid] * dot(middle, table_cols[:, mid])

    def drain(plane, carry):
        wait_send(plane, range(10))
        return carry

    lax.fori_loop(0, PLANES, drain, 0)
    for side in range(2):
        @pl.when(exists[vertical[side]] & far)
        def _(side=side):
            diagonal(side).wait_send()


    for side, cols in ((1, head), (0, tail)):
        @pl.when(receives(side, 2))
        def _(side=side, cols=cols):
            strip(side, mid, 2).wait_recv()
            real[mid, cols] += strip_in[side, mid, :].astype(F32)

    for side, rows in enumerate((tail, head)):
        @pl.when(exists[opposite[vertical[side]]] & far)
        def _(side=side):
            corner(side).wait_recv()

        for here, cols in ((even, head), (odd, tail)):
            @pl.when(exists[opposite[vertical[side]]] & far & here)
            def _(side=side, rows=rows, cols=cols):
                real[rows, cols] += corner_in[side].astype(F32)

    for side, rows in enumerate((tail, head)):
        @pl.when(exists[opposite[vertical[side]]])
        def _(side=side, rows=rows):
            for part in range(2):
                band(side, part).wait_recv()
            for part, cols in enumerate((head, tail)):
                real[rows, cols] += row_in[side, part].astype(F32)

    out_ref[...] = real[mid, mid]

    for side in range(2):
        for rows, number in pieces:
            @pl.when(sends(side, number))
            def _(side=side, rows=rows, number=number):
                strip(side, rows, number).wait_send()

        @pl.when(exists[vertical[side]])
        def _(side=side):
            for part in range(2):
                band(side, part).wait_send()

        @pl.when(exists[vertical[side]] & far)
        def _(side=side):
            corner(side).wait_send()


def shards(n_dec, n_ra, constants, split_maps, white_noise):
    splits, core = split_maps.shape[0], split_maps.shape[1]
    length, half, margin = 2 * core, core, core // 2
    as_bf16 = lambda values: jnp.asarray(np.asarray(values, np.float32).astype(jnp.bfloat16))
    as_f32 = lambda values: jnp.asarray(np.asarray(values, np.float32))
    packed = as_bf16(constants["packed"])
    turned = as_bf16(constants["packed"].T)
    table_cols = as_bf16(constants["packed_cols"])
    turned_cols = as_bf16(constants["packed_cols"].T)
    scale = WEIGHT / ((splits - 1) * constants["total"] * (2 * SMOOTH + 1) ** 2)
    in_vmem = pl.BlockSpec(memory_space=pltpu.VMEM)
    in_hbm = pl.BlockSpec(memory_space=pl.ANY)
    result = pl.pallas_call(
        functools.partial(kernel, n_dec, n_ra, scale**0.5),
        out_shape=pltpu.VMEM((core, core), F32),
        in_specs=[in_hbm] * 12,
        out_specs=in_vmem,
        scratch_shapes=[
            pltpu.VMEM((splits, core, core), BF16),
            pltpu.VMEM((length, length), BF16),
            pltpu.VMEM((length, length), BF16),
            pltpu.VMEM((length, length), BF16),
            pltpu.VMEM((length, length), BF16),
            pltpu.VMEM((length, length), BF16),
            pltpu.VMEM((half + PAD, half), BF16),
            pltpu.VMEM((length, length), BF16),
            pltpu.VMEM((PAD, PAD), BF16),
            pltpu.VMEM((2 * PAD, 2 * PAD), BF16),
            pltpu.VMEM((length, 1), F32),
            pltpu.VMEM((1, length), F32),
            pltpu.VMEM((PLANES, 4, length, margin), BF16),
            pltpu.VMEM((length, length), F32),
            pltpu.VMEM((half, length), F32),
            pltpu.VMEM((PAD, length), F32),
            pltpu.VMEM((half, 256), F32),
            pltpu.VMEM((2, length, half), F32),
            pltpu.VMEM((2, length, half), F32),
            pltpu.VMEM((4, half, half), F32),
            pltpu.VMEM((2, half, 128), F32),
            pltpu.VMEM((8, length), F32),
            pltpu.VMEM((length, length), F32),
            pltpu.VMEM((2, length, margin), BF16),
            pltpu.VMEM((2, length, margin), BF16),
            pltpu.VMEM((2, 2, margin, margin), BF16),
            pltpu.VMEM((2, 2, margin, margin), BF16),
            pltpu.VMEM((2, margin, margin), BF16),
            pltpu.SemaphoreType.DMA((14,)),
            pltpu.SemaphoreType.DMA((PLANES, 10)),
            pltpu.SemaphoreType.DMA((PLANES, 10)),
            pltpu.SemaphoreType.DMA((2, 6)),
            pltpu.SemaphoreType.DMA((2, 6)),
            pltpu.SemaphoreType.DMA((2,)),
        ],
        compiler_params=pltpu.CompilerParams(
            collective_id=0, has_side_effects=True, vmem_limit_bytes=56 << 20
        ),
    )(
        split_maps, white_noise, packed, turned, table_cols, turned_cols,
        as_bf16(constants["smooth_rows"]), as_bf16(constants["smooth_cols"]),
        as_bf16(constants["fold_first"]), as_bf16(constants["fold_last"]),
        as_f32(constants["profile"][:, None]), as_f32(constants["profile"][None, :]),
    )
    return result * (1.0 / (length * length))


def solution(mesh):
    n_dec, n_ra = mesh.shape["dec"], mesh.shape["ra"]

    def body(split_maps, white_noise):
        constants = make_constants(2 * split_maps.shape[1])
        return shards(n_dec, n_ra, constants, split_maps, white_noise)

    placed = (P(None, "dec", "ra"), P("dec", "ra"))
    return jax.shard_map(
        body, mesh=mesh, in_specs=placed, out_specs=P("dec", "ra"), check_vma=False
    )
```

```python
import functools

import jax
import jax.numpy as jnp
import numpy as np
from jax import lax
from jax.experimental import pallas as pl
from jax.experimental.pallas import tpu as pltpu
from jax.sharding import PartitionSpec as P

SMOOTH = 4
MESH = pl.DeviceIdType.MESH
F32 = jnp.float32
BF16 = jnp.bfloat16
PAD = 16


def make_constants(length):
    half = length // 2
    indices = np.arange(length)
    angles = (indices[:, None] * indices[None, :] % length) * (2.0 * np.pi / length)
    cos_table, sin_table = np.cos(angles), np.sin(angles)
    packed = np.concatenate([cos_table[: half + 1], sin_table[1:half]], axis=0)
    profile = np.sin(np.pi * (indices + 0.5) / length) ** 2

    def near(left, right):
        distance = np.abs(left[:, None] - right[None, :]) % length
        return (np.minimum(distance, length - distance) <= SMOOTH).astype(np.float64)

    parity = np.concatenate([np.arange(0, half, 2), np.arange(1, half, 2)])
    order = np.concatenate([parity, half + parity])
    signed = np.concatenate([np.arange(half + 1), -np.arange(1, half)])[order]
    kept = np.arange(half + PAD)
    smooth_rows = near(kept, np.arange(half)) * (kept <= half)[:, None]
    first = np.arange(PAD)
    fold_first = near(first, -first) * (first > 0)[None, :]
    last = half - PAD + np.arange(2 * PAD)
    fold_last = np.zeros((2 * PAD, 2 * PAD))
    fold_last[:, :PAD] = near(last, -last[:PAD])
    fold_last[:, PAD] = near(last, np.array([half]))[:, 0]
    fold_last[last > half] = 0.0
    return dict(
        packed=packed, packed_cols=packed[order], profile=profile, smooth_cols=near(signed, signed), smooth_rows=smooth_rows,
        fold_first=fold_first, fold_last=fold_last, total=float(np.sum(profile**2) ** 2),
    )


def dot(left, right):
    return jnp.dot(left, right, preferred_element_type=F32)


def parts_of(values):
    high = values.astype(BF16)
    return high, (values - high.astype(F32)).astype(BF16)


def fine_left(matrix, values):
    high, low = parts_of(values)
    return dot(matrix, high) + dot(matrix, low)


def fine_right(values, matrix):
    high, low = parts_of(values)
    return dot(high, matrix) + dot(low, matrix)


def contrast(number, planes):
    if number < 3:
        return planes[2 * number] - planes[2 * number + 1]
    pair = [planes[2 * i] + planes[2 * i + 1] for i in range(3)]
    if number == 3:
        return (pair[0] - pair[1]) * 0.5**0.5
    return (pair[0] + pair[1] - 2.0 * pair[2]) * (1.0 / 6.0) ** 0.5


WEIGHT = 0.5
PLANES = 5


def first_lane(rows, cols):
    return lax.broadcasted_iota(jnp.int32, (rows, cols), 1) == 0


def first_row(rows, cols):
    return lax.broadcasted_iota(jnp.int32, (rows, cols), 0) == 0


def edge_line(squares):
    half = squares.shape[1] // 2
    lane = first_lane(squares.shape[0], half)
    left, right = squares[:, :half], squares[:, half:]
    both = left + right
    return jnp.concatenate([jnp.where(lane, left, both), jnp.where(lane, right, both)], axis=1)


def mirrored_cols(values):
    half = values.shape[1] // 2
    lane = first_lane(values.shape[0], half)
    left, right = values[:, :half], values[:, half:]
    return jnp.concatenate([jnp.where(lane, left, right), jnp.where(lane, right, left)], axis=1)


def gains(power, edge_rows, edge_cols, smooth_rows, smooth_cols, fold_first, fold_last):
    half = power.shape[0]
    lane = first_lane(half, 128)
    whole = jnp.concatenate(
        [
            jnp.where(lane, edge_cols[:, :128], power[:, :128]), power[:, 128:half],
            jnp.where(lane, edge_cols[:, 128:], power[:, half : half + 128]), power[:, half + 128 :],
        ],
        axis=1,
    )
    top = jnp.where(first_row(8, 2 * half), edge_line(edge_rows[:8]), whole[:8])
    nyquist = edge_line(edge_rows[8:])
    whole = jnp.concatenate([top, whole[8:], nyquist, jnp.zeros_like(nyquist)], axis=0)
    once = fine_right(whole, smooth_cols)
    smooth = fine_left(smooth_rows, once[:half])
    start = smooth[:PAD] + fine_left(fold_first, mirrored_cols(once[:PAD]))
    tail = jnp.concatenate([mirrored_cols(once[half - PAD : half]), once[half:]], axis=0)
    end = smooth[half - PAD :] + fine_left(fold_last, tail)
    return jnp.sqrt(jnp.concatenate([start, smooth[PAD : half - PAD], end[: PAD + 8]], axis=0))


def combine(noise, factor, sums, edge, last):
    half = noise.shape[0] // 2
    values = noise * factor
    a, b = values[:half, :half], values[:half, half:]
    d, e = values[half:, :half], values[half:, half:]
    rows, lane = first_row(half, half), first_lane(half, half)
    either, both = rows | lane, rows & lane
    zero = jnp.zeros_like(a)
    sums[0] = jnp.where(both, a, 2.0 * (a - jnp.where(either, zero, e)))
    sums[1] = 2.0 * (jnp.where(lane, zero, b) + jnp.where(rows, zero, d))
    sums[2] = jnp.where(either, zero, 2.0 * (a + e))
    sums[3] = jnp.where(either, zero, 2.0 * (b - d))
    edge[0] = jnp.where(both, b, 2.0 * b)[:, :128]
    edge[1] = (2.0 * e)[:, :128]
    bottom = values[half : half + 8]
    single = first_lane(8, half)
    single = jnp.concatenate([single, single], axis=1)
    last[...] = jnp.where(single, bottom, 2.0 * bottom)


def shaped(gain, sums, edge, last):
    half = sums.shape[1]
    plus, minus = gain[:half, :half], gain[:half, half:]
    lane = first_lane(half, 128)
    row = first_row(8, half)
    line = gain[half : half + 8] * last[...]

    def with_lane(values, fixed):
        return jnp.concatenate([jnp.where(lane, minus[:, :128] * fixed, values[:, :128]), values[:, 128:]], axis=1)

    def with_row(values, fixed):
        return jnp.concatenate([jnp.where(row, fixed, values[:8]), values[8:]], axis=0)

    real_plus, imag_plus = plus * sums[0], plus * sums[1]
    real_minus, imag_minus = (minus * sums[2]).astype(BF16), (minus * sums[3]).astype(BF16)
    return (
        jnp.concatenate([real_plus.astype(BF16), with_lane(imag_plus, edge[0]).astype(BF16)], axis=1),
        jnp.concatenate(
            [
                with_row(imag_plus, line[:, :half]).astype(BF16),
                with_row(with_lane(-real_plus, edge[1]), line[:, half:]).astype(BF16),
            ],
            axis=1,
        ),
        jnp.concatenate([real_minus, imag_minus], axis=1),
        jnp.concatenate([-imag_minus, real_minus], axis=1),
    )


def kernel(
    n_dec, n_ra, factor,
    maps_hbm, noise_hbm, table_hbm, turned_hbm, table_cols_hbm, turned_cols_hbm, rows_hbm, cols_hbm, first_hbm, last_hbm,
    tall_hbm, wide_hbm,
    out_ref,
    maps, noise, table, turned, table_cols, turned_cols, smooth_rows, smooth_cols, fold_first, fold_last,
    tall_ref, wide_ref,
    ext, window, power, edge_rows, edge_cols, inner_part, outer_part, sums, edge, last, real,
    strip_out, strip_in, row_out, row_in, corner_in,
    local_sem, send_sem, recv_sem, fold_send, fold_recv, diagonal_sem,
):
    dec, ra = lax.axis_index("dec"), lax.axis_index("ra")
    length = noise.shape[0]
    core = length // 2
    margin = core // 2
    half = core
    low, mid, high = pl.ds(0, margin), pl.ds(margin, core), pl.ds(margin + core, margin)
    head, tail = pl.ds(margin, margin), pl.ds(core, margin)
    exists = {"up": dec > 0, "down": dec < n_dec - 1, "left": ra > 0, "right": ra < n_ra - 1}
    target = {
        "up": {"dec": dec - 1}, "down": {"dec": dec + 1},
        "left": {"ra": ra - 1}, "right": {"ra": ra + 1},
    }
    opposite = {"up": "down", "down": "up", "left": "right", "right": "left"}
    odd = ra % 2 == 1
    even = jnp.logical_not(odd)
    first = jnp.where(odd, 1, 0)
    far = jnp.where(odd, exists["right"], exists["left"])
    across = {"ra": jnp.where(odd, ra + 1, ra - 1)}

    pairs = [
        pltpu.make_async_copy(maps_hbm.at[pl.ds(2 * i, 2)], maps.at[pl.ds(2 * i, 2)], local_sem.at[i])
        for i in range(3)
    ]
    loads = [
        pltpu.make_async_copy(source, place, local_sem.at[3 + number])
        for number, (source, place) in enumerate(
            [(tall_hbm, tall_ref), (wide_hbm, wide_ref), (noise_hbm, noise), (table_hbm, table),
             (turned_cols_hbm, turned_cols), (turned_hbm, turned), (table_cols_hbm, table_cols),
             (rows_hbm, smooth_rows), (cols_hbm, smooth_cols), (first_hbm, fold_first), (last_hbm, fold_last)]
        )
    ]
    for load in pairs:
        load.start()

    barrier = pltpu.get_barrier_semaphore()
    for way in exists:
        @pl.when(exists[way])
        def _(way=way):
            pl.semaphore_signal(barrier, inc=1, device_id=target[way], device_id_type=MESH)
    inner = pl.ds(1, 2)
    moves = [
        ("up", head, 1, high, 1), ("down", tail, 1, low, 1),
        ("up", head, 2, high, 2), ("down", tail, 2, low, 2),
        ("left", mid, 1, mid, 3), ("right", mid, 2, mid, 0),
        ("left", high, 1, high, 3), ("left", low, 1, low, 3),
        ("right", high, 2, high, 0), ("right", low, 2, low, 0),
    ]

    def move(plane, number):
        way, rows, blocks, to_rows, to_blocks = moves[number]
        return pltpu.make_async_remote_copy(
            src_ref=ext.at[plane, blocks, rows, :],
            dst_ref=ext.at[plane, to_blocks, to_rows, :],
            send_sem=send_sem.at[plane, number],
            recv_sem=recv_sem.at[plane, number],
            device_id=target[way],
            device_id_type=MESH,
        )

    vertical = ("up", "down")
    near_first = (((0, 1), odd), ((2, 3), even), ((0, 1), even), ((2, 3), odd))

    def leaves(plane, number):
        way = moves[number][0]
        if number < 6:
            return exists[way]
        return exists[way] & ((odd if way == "left" else even) | (plane < PLANES - 1))

    def arrives(plane, number):
        way = moves[number][0]
        if number < 6:
            return exists[opposite[way]]
        source = exists["down" if number % 2 == 0 else "up"]
        return exists[opposite[way]] & ((even if way == "left" else odd) | source | (plane < PLANES - 1))

    def diagonal(side):
        return pltpu.make_async_remote_copy(
            src_ref=ext.at[PLANES - 1, 1 + first, (head, tail)[side], :],
            dst_ref=ext.at[PLANES - 1, 3 - 3 * first, (high, low)[side], :],
            send_sem=diagonal_sem.at[side],
            recv_sem=recv_sem.at[PLANES - 1, 6 + 2 * first + side],
            device_id={**target[vertical[side]], **across},
            device_id_type=MESH,
        )

    def start(plane, numbers, here=True):
        for number in numbers:
            @pl.when(leaves(plane, number) & here)
            def _(number=number):
                move(plane, number).start()

    def wait_recv(plane, numbers, here=True):
        for number in numbers:
            @pl.when(arrives(plane, number) & here)
            def _(number=number):
                move(plane, number).wait_recv()

    def wait_send(plane, numbers):
        for number in numbers:
            @pl.when(leaves(plane, number))
            def _(number=number):
                move(plane, number).wait_send()

    for plane in range(PLANES):
        if plane < 3:
            pairs[plane].wait()
        used = range(6) if plane >= 3 else range(2 * plane, 2 * plane + 2)
        values = contrast(plane, {s: maps[s].astype(F32) for s in used}).astype(BF16)
        ext[plane, 1, mid, :] = values[:, :margin]
        ext[plane, 2, mid, :] = values[:, margin:]
        if plane == 0:
            pl.semaphore_wait(barrier, sum(here.astype(jnp.int32) for here in exists.values()))
        if plane < PLANES - 1:
            start(plane, (0, 3, 2, 1, 4, 5))
        else:
            for numbers, here in near_first:
                start(plane, numbers, here)
            start(plane, (4, 5))

    for load in loads:
        load.start()
    whole = pl.ds(0, length)
    for way, rows, blocks in (
        ("up", low, inner), ("down", high, inner), ("left", whole, pl.ds(0, 1)), ("right", whole, pl.ds(3, 1)),
    ):
        @pl.when(jnp.logical_not(exists[way]))
        def _(rows=rows, blocks=blocks):
            ext[:, blocks, rows, :] = jnp.zeros((PLANES, blocks.size, rows.size, margin), BF16)

    for way, rows in (("up", low), ("down", high)):
        for here, block in ((even, 0), (odd, 3)):
            @pl.when(jnp.logical_not(exists[way]) & far & here)
            def _(rows=rows, block=block):
                ext[PLANES - 1, block, rows, :] = jnp.zeros((margin, margin), BF16)

    for load in loads[:5]:
        load.wait()
    window[...] = tall_ref[...] * wide_ref[...]
    for total in (power, edge_rows, edge_cols):
        total[...] = jnp.zeros_like(total)

    combine(
        dot(dot(table[...], noise[...]).astype(BF16), turned_cols[...]), factor, sums, edge, last
    )

    def spectra(left, right):
        even_cols = jnp.concatenate([turned_cols[:half, :margin], turned_cols[:half, half : half + margin]], axis=1)
        odd_cols = jnp.concatenate([turned_cols[:half, margin:half], turned_cols[:half, half + margin :]], axis=1)
        evens = dot((left + right).astype(BF16), even_cols)
        odds = dot((left - right).astype(BF16), odd_cols)
        return jnp.concatenate([evens[:, :margin], odds[:, :margin], evens[:, margin:], odds[:, margin:]], axis=1)

    def forward_corners(plane):
        for number in (0, 3, 2, 1):
            wait_recv(plane, (number,))
            start(plane, (6 + number,))

    def windowed(plane, rows, blocks):
        tile = jnp.concatenate([ext[plane, block, rows, :] for block in blocks], axis=1)
        shape = jnp.concatenate(
            [window[rows, block * margin : (block + 1) * margin] for block in blocks], axis=1
        )
        return (shape * tile.astype(F32)).astype(BF16)

    def gather_power(plane):
        wait_recv(plane, range(4, 10))
        halves = dot(table[...], windowed(plane, whole, range(4)))
        add_power(spectra(halves[:, :half], halves[:, half:]))

    def outer_rows(values):
        return jnp.concatenate([values(low), values(high)], axis=0)

    def gather_inner(plane, slot):
        inner_part[slot] = dot(table[...], windowed(plane, whole, (1, 2)))
        wait_recv(plane, (4, 5))
        outer_part[slot] = dot(table[:, mid], windowed(plane, mid, (0, 3)))

    def gather_outer(plane, slot):
        wait_recv(plane, range(6, 10))
        corners = outer_rows(lambda rows: windowed(plane, rows, (0, 3)))
        outer_table = jnp.concatenate([table[:, low], table[:, high]], axis=1)
        sides = outer_part[slot] + dot(outer_table, corners)
        left = jnp.concatenate([sides[:, :margin], inner_part[slot, :, :margin]], axis=1)
        right = jnp.concatenate([inner_part[slot, :, margin:], sides[:, margin:]], axis=1)
        add_power(spectra(left, right))

    def add_power(values):
        a, b = values[:half, :half], values[:half, half:]
        d, e = values[half:, :half], values[half:, half:]
        square = lambda part: part * part
        power[:, :half] += square(a - e) + square(b + d)
        power[:, half:] += square(a + e) + square(b - d)
        edge_rows[:8] += square(values[:8])
        edge_rows[8:] += square(values[half : half + 8])
        edge_cols[:, :128] += square(a[:, :128]) + square(d[:, :128])
        edge_cols[:, 128:] += square(b[:, :128]) + square(e[:, :128])

    forward_corners(0)
    forward_corners(1)
    forward_corners(2)
    gather_power(0)
    for side in range(2):
        @pl.when(exists[vertical[side]] & far)
        def _(side=side):
            diagonal(side).start()

    forward_corners(3)

    def catch_up(plane, carry):
        gather_power(plane)
        return carry

    lax.fori_loop(1, 2, catch_up, 0)
    gather_inner(PLANES - 2, 0)
    for numbers, here in near_first:
        for number in numbers:
            wait_recv(PLANES - 1, (number,), here)
            start(PLANES - 1, (6 + number,), here)
    gather_power(2)
    gather_inner(PLANES - 1, 1)
    for load in loads[5:]:
        load.wait()
    gather_outer(PLANES - 2, 0)
    gather_outer(PLANES - 1, 1)

    gain = gains(
        power[...], edge_rows[...], edge_cols[...], smooth_rows[...], smooth_cols[...],
        fold_first[...], fold_last[...],
    )
    mixed = jnp.concatenate(shaped(gain, sums, edge, last), axis=0)

    def inverse(rows):
        return dot(jnp.concatenate([rows, rows], axis=1), mixed).astype(BF16)

    def strip(side, rows, number):
        return pltpu.make_async_remote_copy(
            src_ref=strip_out.at[side, rows, :],
            dst_ref=strip_in.at[side, rows, :],
            send_sem=fold_send.at[side, number],
            recv_sem=fold_recv.at[side, number],
            device_id=target[("left", "right")[side]],
            device_id_type=MESH,
        )

    def band(side, part):
        return pltpu.make_async_remote_copy(
            src_ref=row_out.at[side, part],
            dst_ref=row_in.at[side, part],
            send_sem=fold_send.at[side, 3 + part],
            recv_sem=fold_recv.at[side, 3 + part],
            device_id=target[vertical[side]],
            device_id_type=MESH,
        )

    def corner(side):
        return pltpu.make_async_remote_copy(
            src_ref=strip_out.at[jnp.where(odd, 1, 0), (low, high)[side], :],
            dst_ref=corner_in.at[side],
            send_sem=fold_send.at[side, 5],
            recv_sem=fold_recv.at[side, 5],
            device_id={**target[vertical[side]], **across},
            device_id_type=MESH,
        )

    pieces = ((low, 0), (high, 1), (mid, 2))
    ways = ("left", "right")

    def sends(side, number):
        return exists[ways[side]] & (True if number == 2 else (odd, even)[side])

    def receives(side, number):
        return exists[opposite[ways[side]]] & (True if number == 2 else (even, odd)[side])
    side_table = jnp.concatenate([table_cols[:, low], table_cols[:, high]], axis=1)

    def put_strips(number, blocks):
        rows = pieces[number][0]
        for side, cols in enumerate((low, high)):
            strip_out[side, rows, :] = (window[rows, cols] * blocks[side]).astype(BF16)

            @pl.when(sends(side, number))
            def _(side=side):
                strip(side, rows, number).start()

    outer = inverse(outer_rows(lambda rows: turned[rows, :]))
    values = dot(outer, table_cols[...])
    for number, (rows, _) in enumerate(pieces[:2]):
        block = values[number * margin : (number + 1) * margin]
        put_strips(number, (block[:, :margin], block[:, margin + core :]))

        @pl.when(exists[vertical[number]] & far)
        def _(number=number):
            corner(number).start()

        for part, cols in enumerate((head, tail)):
            inside = window[rows, cols] * block[:, margin * (1 + part) : margin * (2 + part)]
            real[rows, cols] = inside
            row_out[number, part] = inside.astype(BF16)

        @pl.when(exists[vertical[number]])
        def _(number=number):
            band(number, first).start()

    for number, (rows, _) in enumerate(pieces[:2]):
        for side, part, cols in ((1, 0, head), (0, 1, tail)):
            @pl.when(receives(side, number))
            def _(side=side, part=part, cols=cols, rows=rows, number=number):
                strip(side, rows, number).wait_recv()
                row_out[number, part] = (real[rows, cols] + strip_in[side, rows, :].astype(F32)).astype(BF16)

        @pl.when(exists[vertical[number]])
        def _(number=number):
            band(number, 1 - first).start()

    middle = inverse(turned[mid, :])
    values = dot(middle, side_table)
    put_strips(2, (values[:, :margin], values[:, margin:]))
    real[mid, mid] = window[mid, mid] * dot(middle, table_cols[:, mid])

    def drain(plane, carry):
        wait_send(plane, range(10))
        return carry

    lax.fori_loop(0, PLANES, drain, 0)
    for side in range(2):
        @pl.when(exists[vertical[side]] & far)
        def _(side=side):
            diagonal(side).wait_send()


    for side, cols in ((1, head), (0, tail)):
        @pl.when(receives(side, 2))
        def _(side=side, cols=cols):
            strip(side, mid, 2).wait_recv()
            real[mid, cols] += strip_in[side, mid, :].astype(F32)

    for side, rows in enumerate((tail, head)):
        @pl.when(exists[opposite[vertical[side]]] & far)
        def _(side=side):
            corner(side).wait_recv()

        for here, cols in ((even, head), (odd, tail)):
            @pl.when(exists[opposite[vertical[side]]] & far & here)
            def _(side=side, rows=rows, cols=cols):
                real[rows, cols] += corner_in[side].astype(F32)

    for side, rows in enumerate((tail, head)):
        @pl.when(exists[opposite[vertical[side]]])
        def _(side=side, rows=rows):
            for part in range(2):
                band(side, part).wait_recv()
            for part, cols in enumerate((head, tail)):
                real[rows, cols] += row_in[side, part].astype(F32)

    out_ref[...] = real[mid, mid]

    for side in range(2):
        for rows, number in pieces:
            @pl.when(sends(side, number))
            def _(side=side, rows=rows, number=number):
                strip(side, rows, number).wait_send()

        @pl.when(exists[vertical[side]])
        def _(side=side):
            for part in range(2):
                band(side, part).wait_send()

        @pl.when(exists[vertical[side]] & far)
        def _(side=side):
            corner(side).wait_send()


def shards(n_dec, n_ra, constants, split_maps, white_noise):
    splits, core = split_maps.shape[0], split_maps.shape[1]
    length, half, margin = 2 * core, core, core // 2
    as_bf16 = lambda values: jnp.asarray(np.asarray(values, np.float32).astype(jnp.bfloat16))
    as_f32 = lambda values: jnp.asarray(np.asarray(values, np.float32))
    packed = as_bf16(constants["packed"])
    turned = as_bf16(constants["packed"].T)
    table_cols = as_bf16(constants["packed_cols"])
    turned_cols = as_bf16(constants["packed_cols"].T)
    scale = WEIGHT / ((splits - 1) * constants["total"] * (2 * SMOOTH + 1) ** 2)
    in_vmem = pl.BlockSpec(memory_space=pltpu.VMEM)
    in_hbm = pl.BlockSpec(memory_space=pl.ANY)
    result = pl.pallas_call(
        functools.partial(kernel, n_dec, n_ra, scale**0.5),
        out_shape=pltpu.VMEM((core, core), F32),
        in_specs=[in_hbm] * 12,
        out_specs=in_vmem,
        scratch_shapes=[
            pltpu.VMEM((splits, core, core), BF16),
            pltpu.VMEM((length, length), BF16),
            pltpu.VMEM((length, length), BF16),
            pltpu.VMEM((length, length), BF16),
            pltpu.VMEM((length, length), BF16),
            pltpu.VMEM((length, length), BF16),
            pltpu.VMEM((half + PAD, half), BF16),
            pltpu.VMEM((length, length), BF16),
            pltpu.VMEM((PAD, PAD), BF16),
            pltpu.VMEM((2 * PAD, 2 * PAD), BF16),
            pltpu.VMEM((length, 1), F32),
            pltpu.VMEM((1, length), F32),
            pltpu.VMEM((PLANES, 4, length, margin), BF16),
            pltpu.VMEM((length, length), F32),
            pltpu.VMEM((half, length), F32),
            pltpu.VMEM((PAD, length), F32),
            pltpu.VMEM((half, 256), F32),
            pltpu.VMEM((2, length, half), F32),
            pltpu.VMEM((2, length, half), F32),
            pltpu.VMEM((4, half, half), F32),
            pltpu.VMEM((2, half, 128), F32),
            pltpu.VMEM((8, length), F32),
            pltpu.VMEM((length, length), F32),
            pltpu.VMEM((2, length, margin), BF16),
            pltpu.VMEM((2, length, margin), BF16),
            pltpu.VMEM((2, 2, margin, margin), BF16),
            pltpu.VMEM((2, 2, margin, margin), BF16),
            pltpu.VMEM((2, margin, margin), BF16),
            pltpu.SemaphoreType.DMA((14,)),
            pltpu.SemaphoreType.DMA((PLANES, 10)),
            pltpu.SemaphoreType.DMA((PLANES, 10)),
            pltpu.SemaphoreType.DMA((2, 6)),
            pltpu.SemaphoreType.DMA((2, 6)),
            pltpu.SemaphoreType.DMA((2,)),
        ],
        compiler_params=pltpu.CompilerParams(
            collective_id=0, has_side_effects=True, vmem_limit_bytes=56 << 20
        ),
    )(
        split_maps, white_noise, packed, turned, table_cols, turned_cols,
        as_bf16(constants["smooth_rows"]), as_bf16(constants["smooth_cols"]),
        as_bf16(constants["fold_first"]), as_bf16(constants["fold_last"]),
        as_f32(constants["profile"][:, None]), as_f32(constants["profile"][None, :]),
    )
    return result * (1.0 / (length * length))


def solution(mesh):
    n_dec, n_ra = mesh.shape["dec"], mesh.shape["ra"]

    def body(split_maps, white_noise):
        constants = make_constants(2 * split_maps.shape[1])
        return shards(n_dec, n_ra, constants, split_maps, white_noise)

    placed = (P(None, "dec", "ra"), P("dec", "ra"))
    return jax.shard_map(
        body, mesh=mesh, in_specs=placed, out_specs=P("dec", "ra"), check_vma=False
    )
```
